128 devices in a mesh: dp: 16 (over y, z), tensor: 8 (over x, core).
Axes of the slice: x: 4, y: 4, z: 4, core: 2. Of those that a mesh axis runs over, the one named last changes fastest.
Arguments:
- grads: bfloat16 [16, 1024, 28672], P('dp', None, 'tensor'), may hold values from -6 to 6
- errors: bfloat16 [16, 1024, 28672], P('dp', None, 'tensor'), may hold values from -4 to 4
- basis: float32 [28672, 32], P('tensor'), may hold values from -6 to 6
Outputs:
- new_errors: bfloat16 [16, 1024, 28672], P('dp', None, 'tensor')
- p_basis: float32 [1024, 32], P('tensor')
- q_basis: float32 [28672, 32], P('tensor')
The draws below stay inside these ranges and needn't reach their ends.
All inputs are finite; a program needn't handle non-finite values.
Results may differ from the reference program's by a relative error of at most 0.014.
Values may be sent and summed in bfloat16 or wider, within the bound.
No kernel may reach another device: no remote copies, remote signals or barrier semaphores. Data moves between devices by JAX's collectives and lax.ppermute only.
A program may use at most 64 MiB of HBM per device.

```python
import jax
import jax.numpy as jnp
from jax import lax

ROWS = 1024
FF = 28672
RANK = 32
N_DP = 16


def steps_of(key, dims, cuts, least, high):
    gain = 1.0
    for axis_at, shards_of in cuts:
        draws = jax.random.uniform(jax.random.fold_in(jax.random.fold_in(key, 6), axis_at), (shards_of,), jnp.float32, least / len(cuts), high / len(cuts))
        gain = gain * jnp.repeat(jnp.exp(draws), dims[axis_at] // shards_of).reshape((-1,) + (1,) * (len(dims) - 1 - axis_at))
    return gain


def bell_draw(stream_key, extent, spread, reach, split=(), kind=jnp.bfloat16):
    drawn = jax.random.normal(stream_key, extent, jnp.float32) * spread
    if len(split) > 0:
        drawn = steps_of(stream_key, extent, split, -0.22, 0.18) * drawn
    return jnp.clip(drawn, min=-reach, max=reach).astype(kind)


def setup_inputs(seed: int = 0) -> dict:
    streams_of = jax.random.split(jax.random.key(seed), 4)
    grads = bell_draw(streams_of[0], (N_DP, ROWS, FF), 1.0, 6.0, ((0, 16), (2, 8)))
    errors = bell_draw(streams_of[1], (N_DP, ROWS, FF), 0.5, 4.0, ((0, 16), (2, 8)))
    basis = bell_draw(streams_of[2], (FF, RANK), 1.0, 6.0, ((0, 8),), jnp.float32)
    return dict(grads=grads, errors=errors, basis=basis)


def combined(grads, errors, index):
    return (grads[index].astype(jnp.float32) + errors[index].astype(jnp.float32)).astype(jnp.bfloat16)

def reference(grads, errors, basis):
    basis_b = basis.astype(jnp.bfloat16)
    replicas = jnp.arange(N_DP)

    def forward(index):
        return jnp.dot(combined(grads, errors, index).astype(jnp.float32), basis_b.astype(jnp.float32), preferred_element_type=jnp.float32)
    p_sum = jnp.sum(lax.map(forward, replicas), axis=0)
    gram = jnp.dot(p_sum.T, p_sum, precision=lax.Precision.HIGHEST)
    lower = jnp.linalg.cholesky(gram)
    p_basis = jax.scipy.linalg.solve_triangular(lower, p_sum.T, lower=True).T
    p_b = p_basis.astype(jnp.bfloat16)

    def backward(index):
        return jnp.dot(combined(grads, errors, index).T.astype(jnp.float32), p_b.astype(jnp.float32), preferred_element_type=jnp.float32)
    q_basis = jnp.sum(lax.map(backward, replicas), axis=0) / N_DP
    approx = jnp.dot(p_b.astype(jnp.float32), q_basis.astype(jnp.bfloat16).T.astype(jnp.float32), preferred_element_type=jnp.float32)

    def leftover(index):
        return (combined(grads, errors, index).astype(jnp.float32) - approx).astype(jnp.bfloat16)
    new_errors = lax.map(leftover, replicas)
    return (new_errors, p_basis, q_basis)
```

```python
import functools

import jax
import jax.numpy as jnp
from jax import lax
from jax.experimental import pallas as pl
from jax.experimental.pallas import tpu as pltpu
from jax.sharding import PartitionSpec as P

BF16, F32 = jnp.bfloat16, jnp.float32
HIGHEST = lax.Precision.HIGHEST
LAST_BY_LAST = (((1,), (1,)), ((), ()))
IN_VMEM = pl.BlockSpec(memory_space=pltpu.VMEM)
IN_HBM = pl.BlockSpec(memory_space=pltpu.HBM)
LANES = 128
CHUNKS = 8


def merge_kernel(grads, errors, basis_t, matrix, partial, held, basis, grad_sems, error_sems, basis_sem):
    rows = matrix.shape[0]
    step = rows // CHUNKS
    pltpu.make_async_copy(basis_t, basis, basis_sem).start()
    for i in range(CHUNKS):
        part = pl.ds(i * step, step)
        pltpu.make_async_copy(grads.at[0, part], matrix.at[part], grad_sems.at[i]).start()
        pltpu.make_async_copy(errors.at[0, part], held.at[part], error_sems.at[i]).start()
    pltpu.make_async_copy(basis_t, basis, basis_sem).wait()
    basis_b = basis[...].astype(BF16)
    for i in range(CHUNKS):
        part = pl.ds(i * step, step)
        pltpu.make_async_copy(grads.at[0, part], matrix.at[part], grad_sems.at[i]).wait()
        pltpu.make_async_copy(errors.at[0, part], held.at[part], error_sems.at[i]).wait()
        total = matrix[part, :] + held[part, :]
        matrix[part, :] = total
        product = lax.dot_general(total, basis_b, LAST_BY_LAST, preferred_element_type=F32)
        partial[i] = product.T


def merge(grads, errors, basis_t):
    rows, cols = grads.shape[1:]
    rank = basis_t.shape[0]
    return pl.pallas_call(
        merge_kernel,
        out_shape=(
            jax.ShapeDtypeStruct((rows, cols), BF16),
            jax.ShapeDtypeStruct((rows // LANES, rank, LANES), F32),
        ),
        in_specs=[IN_HBM] * 3,
        out_specs=(IN_VMEM, IN_VMEM),
        scratch_shapes=[
            pltpu.VMEM((rows, cols), BF16),
            pltpu.VMEM((rank, cols), F32),
            pltpu.SemaphoreType.DMA((CHUNKS,)),
            pltpu.SemaphoreType.DMA((CHUNKS,)),
            pltpu.SemaphoreType.DMA(()),
        ],
        compiler_params=pltpu.CompilerParams(vmem_limit_bytes=24 << 20),
        name="merge",
    )(grads, errors, basis_t)


def inverse_factor(gram):
    rank = gram.shape[0]
    row = lax.broadcasted_iota(jnp.int32, (rank, LANES), 0)
    lane = lax.broadcasted_iota(jnp.int32, (rank, LANES), 1)
    work = jnp.concatenate([gram, jnp.zeros((rank, LANES - rank), F32)], axis=1)
    work = work + jnp.where(lane == row + rank, 1.0, 0.0)
    scale = jnp.zeros((rank, LANES), F32)
    for k in range(rank):
        column = jnp.broadcast_to(work[:, k : k + 1], (rank, LANES))
        pivot_row = jnp.broadcast_to(work[k : k + 1, :], (rank, LANES))
        pivot = jnp.broadcast_to(column[k : k + 1, :], (rank, LANES))
        scale = jnp.where(row == k, pivot, scale)
        work = work - jnp.where(row > k, column / pivot, 0.0) * pivot_row
    return (work * lax.rsqrt(scale))[:, rank : 2 * rank]


def project_kernel(pieces, own, matrix, p_own, p_b, q_pieces, whole):
    blocks, rank, _ = pieces.shape
    for i in range(blocks):
        whole[:, i * LANES : (i + 1) * LANES] = pieces[i]
    p_sum = whole[...]
    gram = lax.dot_general(p_sum, p_sum, LAST_BY_LAST, precision=HIGHEST, preferred_element_type=F32)
    inverse = inverse_factor(gram)
    p_own[...] = jnp.dot(inverse, own[0], precision=HIGHEST, preferred_element_type=F32)
    rounded = jnp.dot(inverse, p_sum, precision=HIGHEST, preferred_element_type=F32).astype(BF16)
    p_b[...] = rounded
    count, height, width = q_pieces.shape
    for j in range(count * height // rank):
        q = jnp.dot(rounded, matrix[:, j * width : (j + 1) * width], preferred_element_type=F32).astype(BF16)
        for s in range(rank // height):
            q_pieces[j * (rank // height) + s] = q[s * height : (s + 1) * height]


def project(pieces, own, matrix, count):
    blocks, rank, _ = pieces.shape
    rows, cols = matrix.shape
    height = 8
    width = cols * rank // (count * height)
    return pl.pallas_call(
        project_kernel,
        out_shape=(
            jax.ShapeDtypeStruct((rank, LANES), F32),
            jax.ShapeDtypeStruct((rank, rows), BF16),
            jax.ShapeDtypeStruct((count, height, width), BF16),
        ),
        in_specs=[IN_VMEM] * 3,
        out_specs=(IN_VMEM,) * 3,
        scratch_shapes=[pltpu.VMEM((rank, rows), F32)],
        compiler_params=pltpu.CompilerParams(vmem_limit_bytes=24 << 20),
        name="project",
    )(pieces, own, matrix)


def subtract_kernel(mean, q_pieces, p_b, matrix, new_errors, q_out, out_buf, q_buf, sems, q_sem):
    rank = p_b.shape[0]
    count, height, width = q_pieces.shape
    rows, cols = matrix.shape
    per = rank // height
    step = rows // CHUNKS
    for j in range(count // per):
        for s in range(per):
            q_buf[s * height : (s + 1) * height, j * width : (j + 1) * width] = (
                q_pieces[j * per + s].astype(F32) * mean
            )
    pltpu.make_async_copy(q_buf, q_out, q_sem).start()
    q_b = q_buf[...].astype(BF16)
    left = p_b[...].T
    for i in range(CHUNKS):
        part = pl.ds(i * step, step)
        approx = jnp.dot(left[i * step : (i + 1) * step], q_b, preferred_element_type=F32)
        out_buf[part, :] = (matrix[part, :].astype(F32) - approx).astype(BF16)
        pltpu.make_async_copy(out_buf.at[part], new_errors.at[0, part], sems.at[i]).start()
    for i in range(CHUNKS):
        part = pl.ds(i * step, step)
        pltpu.make_async_copy(out_buf.at[part], new_errors.at[0, part], sems.at[i]).wait()
    pltpu.make_async_copy(q_buf, q_out, q_sem).wait()


def subtract(q_pieces, p_b, matrix):
    rows, cols = matrix.shape
    rank = p_b.shape[0]
    count = q_pieces.shape[0]
    return pl.pallas_call(
        functools.partial(subtract_kernel, 1.0 / count),
        out_shape=(
            jax.ShapeDtypeStruct((1, rows, cols), BF16),
            jax.ShapeDtypeStruct((rank, cols), F32),
        ),
        in_specs=[IN_VMEM] * 3,
        out_specs=(IN_HBM, IN_HBM),
        scratch_shapes=[
            pltpu.VMEM((rows, cols), BF16),
            pltpu.VMEM((rank, cols), F32),
            pltpu.SemaphoreType.DMA((CHUNKS,)),
            pltpu.SemaphoreType.DMA(()),
        ],
        compiler_params=pltpu.CompilerParams(vmem_limit_bytes=24 << 20),
        name="subtract",
    )(q_pieces, p_b, matrix)


def total_kernel(pieces, copies):
    total = pieces[0].astype(F32)
    for i in range(1, pieces.shape[0]):
        total = total + pieces[i].astype(F32)
    total = total.astype(copies.dtype)
    for i in range(copies.shape[0]):
        copies[i] = total


def summed_copies(pieces, count):
    return pl.pallas_call(
        total_kernel,
        out_shape=jax.ShapeDtypeStruct((count, *pieces.shape[1:]), pieces.dtype),
        in_specs=[IN_VMEM],
        out_specs=IN_VMEM,
        compiler_params=pltpu.CompilerParams(vmem_limit_bytes=4 << 20),
        name="summed_copies",
    )(pieces)


def exchanged(pieces, axis):
    return lax.all_to_all(pieces, axis, split_axis=0, concat_axis=0, tiled=True)


def on_device(grads, errors, basis):
    n_dp, n_tensor = lax.axis_size("dp"), lax.axis_size("tensor")
    matrix, partial = merge(grads, errors, basis.T)
    p_terms = exchanged(summed_copies(exchanged(partial, "tensor"), n_dp), "dp")
    p_copies = summed_copies(p_terms, n_tensor)
    p_own, p_b, q_pieces = project(exchanged(p_copies, "tensor"), p_copies, matrix, n_dp)
    q_sums = exchanged(summed_copies(exchanged(q_pieces, "dp"), n_dp), "dp")
    new_errors, q_out = subtract(q_sums, p_b, matrix)
    return new_errors, p_own.T, q_out.T


def solution(mesh):
    return jax.shard_map(
        on_device,
        mesh=mesh,
        in_specs=(P("dp", None, "tensor"), P("dp", None, "tensor"), P("tensor", None)),
        out_specs=(P("dp", None, "tensor"), P("tensor", None), P("tensor", None)),
        check_vma=False,
    )
```

```python
import functools

import jax
import jax.numpy as jnp
from jax import lax
from jax.experimental import pallas as pl
from jax.experimental.pallas import tpu as pltpu
from jax.sharding import PartitionSpec as P

BF16, F32 = jnp.bfloat16, jnp.float32
HIGHEST = lax.Precision.HIGHEST
LAST_BY_LAST = (((1,), (1,)), ((), ()))
IN_VMEM = pl.BlockSpec(memory_space=pltpu.VMEM)
IN_HBM = pl.BlockSpec(memory_space=pltpu.HBM)
LANES = 128
CHUNKS = 8
WIDTHS = (512, 512, 512, 512, 512, 512, 512)
STARTS = tuple(sum(WIDTHS[:i]) for i in range(len(WIDTHS)))


def merge_kernel(grads, errors, basis_t, matrix, partial, held, grad_sems, error_sems):
    def copies(i):
        part = (slice(None), pl.ds(STARTS[i], WIDTHS[i]))
        return (
            pltpu.make_async_copy(grads.at[(0, *part)], matrix.at[part], grad_sems.at[i]),
            pltpu.make_async_copy(errors.at[(0, *part)], held.at[part], error_sems.at[i]),
        )

    for i in range(len(WIDTHS)):
        for copy in copies(i):
            copy.start()
    basis_b = basis_t[...].astype(BF16)
    for i in range(len(WIDTHS)):
        for copy in copies(i):
            copy.wait()
        part = slice(STARTS[i], STARTS[i] + WIDTHS[i])
        total = matrix[:, part] + held[:, part]
        matrix[:, part] = total
        product = lax.dot_general(basis_b[:, part], total, LAST_BY_LAST, preferred_element_type=F32)
        for j in range(partial.shape[0]):
            term = product[:, j * LANES : (j + 1) * LANES]
            partial[j] = term if i == 0 else partial[j] + term


def merge(grads, errors, basis_t):
    rows, cols = grads.shape[1:]
    rank = basis_t.shape[0]
    return pl.pallas_call(
        merge_kernel,
        out_shape=(
            jax.ShapeDtypeStruct((rows, cols), BF16),
            jax.ShapeDtypeStruct((rows // LANES, rank, LANES), F32),
        ),
        in_specs=[IN_HBM, IN_HBM, IN_VMEM],
        out_specs=(IN_VMEM, IN_VMEM),
        scratch_shapes=[
            pltpu.VMEM((rows, cols), BF16),
            pltpu.SemaphoreType.DMA((len(WIDTHS),)),
            pltpu.SemaphoreType.DMA((len(WIDTHS),)),
        ],
        compiler_params=pltpu.CompilerParams(vmem_limit_bytes=44 << 20),
        name="merge",
    )(grads, errors, basis_t)


def inverse_factor(gram):
    rank = gram.shape[0]
    row = lax.broadcasted_iota(jnp.int32, (rank, LANES), 0)
    lane = lax.broadcasted_iota(jnp.int32, (rank, LANES), 1)
    work = jnp.concatenate([gram, jnp.zeros((rank, LANES - rank), F32)], axis=1)
    work = work + jnp.where(lane == row + rank, 1.0, 0.0)
    scale = jnp.zeros((rank, LANES), F32)
    for k in range(rank):
        column = jnp.broadcast_to(work[:, k : k + 1], (rank, LANES))
        pivot_row = jnp.broadcast_to(work[k : k + 1, :], (rank, LANES))
        pivot = jnp.broadcast_to(column[k : k + 1, :], (rank, LANES))
        scale = jnp.where(row == k, pivot, scale)
        work = work - jnp.where(row > k, column / pivot, 0.0) * pivot_row
    return (work * lax.rsqrt(scale))[:, rank : 2 * rank]


def project_kernel(pieces, own, matrix, p_own, p_b, q_pieces, whole):
    blocks, rank, _ = pieces.shape
    for i in range(blocks):
        whole[:, i * LANES : (i + 1) * LANES] = pieces[i]
    p_sum = whole[...]
    gram = lax.dot_general(p_sum, p_sum, LAST_BY_LAST, precision=HIGHEST, preferred_element_type=F32)
    inverse = inverse_factor(gram)
    p_own[...] = jnp.dot(inverse, own[0], precision=HIGHEST, preferred_element_type=F32)
    rounded = jnp.dot(inverse, p_sum, precision=HIGHEST, preferred_element_type=F32).astype(BF16)
    p_b[...] = rounded
    count, height, width = q_pieces.shape
    for j in range(count * height // rank):
        q = jnp.dot(rounded, matrix[:, j * width : (j + 1) * width], preferred_element_type=F32).astype(BF16)
        for s in range(rank // height):
            q_pieces[j * (rank // height) + s] = q[s * height : (s + 1) * height]


def project(pieces, own, matrix, count):
    blocks, rank, _ = pieces.shape
    rows, cols = matrix.shape
    height = 8
    width = cols * rank // (count * height)
    return pl.pallas_call(
        project_kernel,
        out_shape=(
            jax.ShapeDtypeStruct((rank, LANES), F32),
            jax.ShapeDtypeStruct((rank, rows), BF16),
            jax.ShapeDtypeStruct((count, height, width), BF16),
        ),
        in_specs=[IN_VMEM] * 3,
        out_specs=(IN_VMEM,) * 3,
        scratch_shapes=[pltpu.VMEM((rank, rows), F32)],
        compiler_params=pltpu.CompilerParams(vmem_limit_bytes=24 << 20),
        name="project",
    )(pieces, own, matrix)


def subtract_kernel(mean, q_pieces, p_b, matrix, new_errors, q_out, out_buf, q_buf, sems, q_sem):
    rank = p_b.shape[0]
    count, height, width = q_pieces.shape
    rows, cols = matrix.shape
    per = rank // height
    step = rows // CHUNKS
    for j in range(count // per):
        for s in range(per):
            q_buf[s * height : (s + 1) * height, j * width : (j + 1) * width] = (
                q_pieces[j * per + s].astype(F32) * mean
            )
    pltpu.make_async_copy(q_buf, q_out, q_sem).start()
    q_b = q_buf[...].astype(BF16)
    left = p_b[...].T
    for i in range(CHUNKS):
        part = pl.ds(i * step, step)
        approx = jnp.dot(left[i * step : (i + 1) * step], q_b, preferred_element_type=F32)
        out_buf[part, :] = (matrix[part, :].astype(F32) - approx).astype(BF16)
        pltpu.make_async_copy(out_buf.at[part], new_errors.at[0, part], sems.at[i]).start()
    for i in range(CHUNKS):
        part = pl.ds(i * step, step)
        pltpu.make_async_copy(out_buf.at[part], new_errors.at[0, part], sems.at[i]).wait()
    pltpu.make_async_copy(q_buf, q_out, q_sem).wait()


def subtract(q_pieces, p_b, matrix):
    rows, cols = matrix.shape
    rank = p_b.shape[0]
    count = q_pieces.shape[0]
    return pl.pallas_call(
        functools.partial(subtract_kernel, 1.0 / count),
        out_shape=(
            jax.ShapeDtypeStruct((1, rows, cols), BF16),
            jax.ShapeDtypeStruct((rank, cols), F32),
        ),
        in_specs=[IN_VMEM] * 3,
        out_specs=(IN_HBM, IN_HBM),
        scratch_shapes=[
            pltpu.VMEM((rows, cols), BF16),
            pltpu.VMEM((rank, cols), F32),
            pltpu.SemaphoreType.DMA((CHUNKS,)),
            pltpu.SemaphoreType.DMA(()),
        ],
        compiler_params=pltpu.CompilerParams(vmem_limit_bytes=24 << 20),
        name="subtract",
    )(q_pieces, p_b, matrix)


def total_kernel(pieces, copies):
    total = pieces[0].astype(F32)
    for i in range(1, pieces.shape[0]):
        total = total + pieces[i].astype(F32)
    total = total.astype(copies.dtype)
    for i in range(copies.shape[0]):
        copies[i] = total


def summed_copies(pieces, count):
    return pl.pallas_call(
        total_kernel,
        out_shape=jax.ShapeDtypeStruct((count, *pieces.shape[1:]), pieces.dtype),
        in_specs=[IN_VMEM],
        out_specs=IN_VMEM,
        compiler_params=pltpu.CompilerParams(vmem_limit_bytes=4 << 20),
        name="summed_copies",
    )(pieces)


def exchanged(pieces, axis):
    return lax.all_to_all(pieces, axis, split_axis=0, concat_axis=0, tiled=True)


def on_device(grads, errors, basis):
    n_dp, n_tensor = lax.axis_size("dp"), lax.axis_size("tensor")
    matrix, partial = merge(grads, errors, basis.T)
    p_terms = exchanged(summed_copies(exchanged(partial, "tensor"), n_dp), "dp")
    p_copies = summed_copies(p_terms, n_tensor)
    p_own, p_b, q_pieces = project(exchanged(p_copies, "tensor"), p_copies, matrix, n_dp)
    q_sums = exchanged(summed_copies(exchanged(q_pieces, "dp"), n_dp), "dp")
    new_errors, q_out = subtract(q_sums, p_b, matrix)
    return new_errors, p_own.T, q_out.T


def solution(mesh):
    return jax.shard_map(
        on_device,
        mesh=mesh,
        in_specs=(P("dp", None, "tensor"), P("dp", None, "tensor"), P("tensor", None)),
        out_specs=(P("dp", None, "tensor"), P("tensor", None), P("tensor", None)),
        check_vma=False,
    )
```

```python
import functools

import jax
import jax.numpy as jnp
from jax import lax
from jax.experimental import pallas as pl
from jax.experimental.pallas import tpu as pltpu
from jax.sharding import PartitionSpec as P

BF16, F32 = jnp.bfloat16, jnp.float32
HIGHEST = lax.Precision.HIGHEST
LAST_BY_LAST = (((1,), (1,)), ((), ()))
IN_VMEM = pl.BlockSpec(memory_space=pltpu.VMEM)
IN_HBM = pl.BlockSpec(memory_space=pltpu.HBM)
LANES = 128
CHUNKS = 16
BLOCK = 8
WIDTHS = (512, 512, 512, 512, 512, 512, 512)
STARTS = tuple(sum(WIDTHS[:i]) for i in range(len(WIDTHS)))


def merge_kernel(grads, errors, basis_t, matrix, partial, held, grad_sems, error_sems):
    def copies(i):
        part = (slice(None), pl.ds(STARTS[i], WIDTHS[i]))
        return (
            pltpu.make_async_copy(grads.at[(0, *part)], matrix.at[part], grad_sems.at[i]),
            pltpu.make_async_copy(errors.at[(0, *part)], held.at[part], error_sems.at[i]),
        )

    for i in range(len(WIDTHS)):
        for copy in copies(i):
            copy.start()
    basis_b = basis_t[...].astype(BF16)
    for i in range(len(WIDTHS)):
        for copy in copies(i):
            copy.wait()
        part = slice(STARTS[i], STARTS[i] + WIDTHS[i])
        total = matrix[:, part] + held[:, part]
        matrix[:, part] = total
        product = lax.dot_general(basis_b[:, part], total, LAST_BY_LAST, preferred_element_type=F32)
        for j in range(partial.shape[0]):
            term = product[:, j * LANES : (j + 1) * LANES]
            partial[j] = term if i == 0 else partial[j] + term


def merge(grads, errors, basis_t):
    rows, cols = grads.shape[1:]
    rank = basis_t.shape[0]
    return pl.pallas_call(
        merge_kernel,
        out_shape=(
            jax.ShapeDtypeStruct((rows, cols), BF16),
            jax.ShapeDtypeStruct((rows // LANES, rank, LANES), F32),
        ),
        in_specs=[IN_HBM, IN_HBM, IN_VMEM],
        out_specs=(IN_VMEM, IN_VMEM),
        scratch_shapes=[
            pltpu.VMEM((rows, cols), BF16),
            pltpu.SemaphoreType.DMA((len(WIDTHS),)),
            pltpu.SemaphoreType.DMA((len(WIDTHS),)),
        ],
        compiler_params=pltpu.CompilerParams(vmem_limit_bytes=44 << 20),
        name="merge",
    )(grads, errors, basis_t)


def inverse_factor(gram):
    rank = gram.shape[0]
    row = lax.broadcasted_iota(jnp.int32, (rank, LANES), 0)
    lane = lax.broadcasted_iota(jnp.int32, (rank, LANES), 1)
    work = jnp.concatenate([gram, jnp.zeros((rank, LANES - rank), F32)], axis=1)
    work = work + jnp.where(lane == row + rank, 1.0, 0.0)
    scale = jnp.zeros((rank, LANES), F32)
    for k in range(0, rank, BLOCK):
        columns = [jnp.broadcast_to(work[:, k + p : k + p + 1], (rank, LANES)) for p in range(BLOCK)]
        lines = [work[k + p : k + p + 1, :] for p in range(BLOCK)]
        scaled = []
        for p in range(BLOCK):
            pivot = columns[p][k + p : k + p + 1, :]
            inverse = 1.0 / pivot
            for q in range(p + 1, BLOCK):
                factor = columns[p][k + q : k + q + 1, :] * inverse
                lines[q] = lines[q] - factor * lines[p]
                columns[q] = columns[q] - factor * columns[p]
            scale = jnp.where(row == k + p, pivot, scale)
            work = jnp.where(row == k + p, lines[p], work)
            scaled.append(lines[p] * inverse)
        for p in range(BLOCK):
            work = work - jnp.where(row >= k + BLOCK, columns[p], 0.0) * scaled[p]
    return (work * lax.rsqrt(scale))[:, rank : 2 * rank]


def project_kernel(pieces, own, matrix, p_own, p_b, q_pieces, whole):
    blocks, rank, _ = pieces.shape
    for i in range(blocks):
        whole[:, i * LANES : (i + 1) * LANES] = pieces[i]
    p_sum = whole[...]
    gram = lax.dot_general(p_sum, p_sum, LAST_BY_LAST, precision=HIGHEST, preferred_element_type=F32)
    inverse = inverse_factor(gram)
    p_own[...] = jnp.dot(inverse, own[0], precision=HIGHEST, preferred_element_type=F32)
    rounded = jnp.dot(inverse, p_sum, precision=HIGHEST, preferred_element_type=F32).astype(BF16)
    p_b[...] = rounded
    count, height, width = q_pieces.shape
    for j in range(count * height // rank):
        q = jnp.dot(rounded, matrix[:, j * width : (j + 1) * width], preferred_element_type=F32).astype(BF16)
        for s in range(rank // height):
            q_pieces[j * (rank // height) + s] = q[s * height : (s + 1) * height]


def project(pieces, own, matrix, count):
    blocks, rank, _ = pieces.shape
    rows, cols = matrix.shape
    height = 8
    width = cols * rank // (count * height)
    return pl.pallas_call(
        project_kernel,
        out_shape=(
            jax.ShapeDtypeStruct((rank, LANES), F32),
            jax.ShapeDtypeStruct((rank, rows), BF16),
            jax.ShapeDtypeStruct((count, height, width), BF16),
        ),
        in_specs=[IN_VMEM] * 3,
        out_specs=(IN_VMEM,) * 3,
        scratch_shapes=[pltpu.VMEM((rank, rows), F32)],
        compiler_params=pltpu.CompilerParams(vmem_limit_bytes=24 << 20),
        name="project",
    )(pieces, own, matrix)


def subtract_kernel(mean, q_pieces, p_b, matrix, new_errors, q_out, out_buf, q_buf, sems, q_sem):
    rank = p_b.shape[0]
    count, height, width = q_pieces.shape
    rows, cols = matrix.shape
    per = rank // height
    step = rows // CHUNKS
    for j in range(count // per):
        for s in range(per):
            q_buf[s * height : (s + 1) * height, j * width : (j + 1) * width] = (
                q_pieces[j * per + s].astype(F32) * mean
            )
    pltpu.make_async_copy(q_buf, q_out, q_sem).start()
    q_b = q_buf[...].astype(BF16)
    left = p_b[...].T
    for i in range(CHUNKS):
        part = pl.ds(i * step, step)
        approx = jnp.dot(left[i * step : (i + 1) * step], q_b, preferred_element_type=F32)
        out_buf[part, :] = (matrix[part, :].astype(F32) - approx).astype(BF16)
        pltpu.make_async_copy(out_buf.at[part], new_errors.at[0, part], sems.at[i]).start()
    for i in range(CHUNKS):
        part = pl.ds(i * step, step)
        pltpu.make_async_copy(out_buf.at[part], new_errors.at[0, part], sems.at[i]).wait()
    pltpu.make_async_copy(q_buf, q_out, q_sem).wait()


def subtract(q_pieces, p_b, matrix):
    rows, cols = matrix.shape
    rank = p_b.shape[0]
    count = q_pieces.shape[0]
    return pl.pallas_call(
        functools.partial(subtract_kernel, 1.0 / count),
        out_shape=(
            jax.ShapeDtypeStruct((1, rows, cols), BF16),
            jax.ShapeDtypeStruct((rank, cols), F32),
        ),
        in_specs=[IN_VMEM] * 3,
        out_specs=(IN_HBM, IN_HBM),
        scratch_shapes=[
            pltpu.VMEM((rows, cols), BF16),
            pltpu.VMEM((rank, cols), F32),
            pltpu.SemaphoreType.DMA((CHUNKS,)),
            pltpu.SemaphoreType.DMA(()),
        ],
        compiler_params=pltpu.CompilerParams(vmem_limit_bytes=24 << 20),
        name="subtract",
    )(q_pieces, p_b, matrix)


def total_kernel(pieces, copies):
    total = pieces[0].astype(F32)
    for i in range(1, pieces.shape[0]):
        total = total + pieces[i].astype(F32)
    total = total.astype(copies.dtype)
    for i in range(copies.shape[0]):
        copies[i] = total


def summed_copies(pieces, count):
    return pl.pallas_call(
        total_kernel,
        out_shape=jax.ShapeDtypeStruct((count, *pieces.shape[1:]), pieces.dtype),
        in_specs=[IN_VMEM],
        out_specs=IN_VMEM,
        compiler_params=pltpu.CompilerParams(vmem_limit_bytes=4 << 20),
        name="summed_copies",
    )(pieces)


def exchanged(pieces, axis):
    return lax.all_to_all(pieces, axis, split_axis=0, concat_axis=0, tiled=True)


def on_device(grads, errors, basis):
    n_dp, n_tensor = lax.axis_size("dp"), lax.axis_size("tensor")
    matrix, partial = merge(grads, errors, basis.T)
    p_terms = exchanged(summed_copies(exchanged(partial, "tensor"), n_dp), "dp")
    p_copies = summed_copies(p_terms, n_tensor)
    p_own, p_b, q_pieces = project(exchanged(p_copies, "tensor"), p_copies, matrix, n_dp)
    q_sums = exchanged(summed_copies(exchanged(q_pieces, "dp"), n_dp), "dp")
    new_errors, q_out = subtract(q_sums, p_b, matrix)
    return new_errors, p_own.T, q_out.T


def solution(mesh):
    return jax.shard_map(
        on_device,
        mesh=mesh,
        in_specs=(P("dp", None, "tensor"), P("dp", None, "tensor"), P("tensor", None)),
        out_specs=(P("dp", None, "tensor"), P("tensor", None), P("tensor", None)),
        check_vma=False,
    )
```

```python
import functools

import jax
import jax.numpy as jnp
from jax import lax
from jax.experimental import pallas as pl
from jax.experimental.pallas import tpu as pltpu
from jax.sharding import PartitionSpec as P

BF16, F32 = jnp.bfloat16, jnp.float32
HIGHEST = lax.Precision.HIGHEST
LAST_BY_LAST = (((1,), (1,)), ((), ()))
IN_VMEM = pl.BlockSpec(memory_space=pltpu.VMEM)
IN_HBM = pl.BlockSpec(memory_space=pltpu.HBM)
LANES = 128
CHUNKS = 16
BLOCK = 8
WIDTHS = (512, 512, 512, 512, 512, 512, 512)
STARTS = tuple(sum(WIDTHS[:i]) for i in range(len(WIDTHS)))


def merge_kernel(grads, errors, basis_t, matrix, partial, held, grad_sems, error_sems):
    def copies(i):
        part = (slice(None), pl.ds(STARTS[i], WIDTHS[i]))
        return (
            pltpu.make_async_copy(grads.at[(0, *part)], matrix.at[part], grad_sems.at[i]),
            pltpu.make_async_copy(errors.at[(0, *part)], held.at[part], error_sems.at[i]),
        )

    for i in range(len(WIDTHS)):
        for copy in copies(i):
            copy.start()
    basis_b = basis_t[...].astype(BF16)
    for i in range(len(WIDTHS)):
        for copy in copies(i):
            copy.wait()
        part = slice(STARTS[i], STARTS[i] + WIDTHS[i])
        total = matrix[:, part] + held[:, part]
        matrix[:, part] = total
        product = lax.dot_general(basis_b[:, part], total, LAST_BY_LAST, preferred_element_type=F32)
        rank = product.shape[0]
        for j in range(product.shape[1] // LANES):
            block = pl.ds(j * rank, rank)
            term = product[:, j * LANES : (j + 1) * LANES]
            partial[block, :] = term if i == 0 else partial[block, :] + term


def merge(grads, errors, basis_t):
    rows, cols = grads.shape[1:]
    rank = basis_t.shape[0]
    return pl.pallas_call(
        merge_kernel,
        out_shape=(
            jax.ShapeDtypeStruct((rows, cols), BF16),
            jax.ShapeDtypeStruct((rows // LANES * rank, LANES), F32),
        ),
        in_specs=[IN_HBM, IN_HBM, IN_VMEM],
        out_specs=(IN_VMEM, IN_VMEM),
        scratch_shapes=[
            pltpu.VMEM((rows, cols), BF16),
            pltpu.SemaphoreType.DMA((len(WIDTHS),)),
            pltpu.SemaphoreType.DMA((len(WIDTHS),)),
        ],
        compiler_params=pltpu.CompilerParams(vmem_limit_bytes=44 << 20),
        name="merge",
    )(grads, errors, basis_t)


def inverse_factor(gram):
    rank = gram.shape[0]
    row = lax.broadcasted_iota(jnp.int32, (rank, LANES), 0)
    lane = lax.broadcasted_iota(jnp.int32, (rank, LANES), 1)
    work = jnp.concatenate([gram, jnp.zeros((rank, LANES - rank), F32)], axis=1)
    work = work + jnp.where(lane == row + rank, 1.0, 0.0)
    scale = jnp.zeros((rank, LANES), F32)
    for k in range(0, rank, BLOCK):
        columns = [jnp.broadcast_to(work[:, k + p : k + p + 1], (rank, LANES)) for p in range(BLOCK)]
        lines = [work[k + p : k + p + 1, :] for p in range(BLOCK)]
        scaled = []
        for p in range(BLOCK):
            pivot = columns[p][k + p : k + p + 1, :]
            inverse = 1.0 / pivot
            for q in range(p + 1, BLOCK):
                factor = columns[p][k + q : k + q + 1, :] * inverse
                lines[q] = lines[q] - factor * lines[p]
                columns[q] = columns[q] - factor * columns[p]
            scale = jnp.where(row == k + p, pivot, scale)
            work = jnp.where(row == k + p, lines[p], work)
            scaled.append(lines[p] * inverse)
        for p in range(BLOCK):
            work = work - jnp.where(row >= k + BLOCK, columns[p], 0.0) * scaled[p]
    return (work * lax.rsqrt(scale))[:, rank : 2 * rank]


def project_kernel(lines, matrix, p_own, p_b, q_pieces, whole):
    rank = whole.shape[0]
    for i in range(lines.shape[0] // rank):
        whole[:, i * LANES : (i + 1) * LANES] = lines[i * rank : (i + 1) * rank]
    p_sum = whole[...]
    gram = lax.dot_general(p_sum, p_sum, LAST_BY_LAST, precision=HIGHEST, preferred_element_type=F32)
    inverse = inverse_factor(gram)
    own = lines[pl.ds(pl.multiple_of(lax.axis_index("tensor") * rank, rank), rank), :]
    p_own[...] = jnp.dot(inverse, own, precision=HIGHEST, preferred_element_type=F32)
    rounded = jnp.dot(inverse, p_sum, precision=HIGHEST, preferred_element_type=F32).astype(BF16)
    p_b[...] = rounded
    count, height, width = q_pieces.shape
    for j in range(count * height // rank):
        q = jnp.dot(rounded, matrix[:, j * width : (j + 1) * width], preferred_element_type=F32).astype(BF16)
        for s in range(rank // height):
            q_pieces[j * (rank // height) + s] = q[s * height : (s + 1) * height]


def project(lines, matrix, count):
    rows, cols = matrix.shape
    rank = lines.size // rows
    height = 8
    width = cols * rank // (count * height)
    return pl.pallas_call(
        project_kernel,
        out_shape=(
            jax.ShapeDtypeStruct((rank, LANES), F32),
            jax.ShapeDtypeStruct((rank, rows), BF16),
            jax.ShapeDtypeStruct((count, height, width), BF16),
        ),
        in_specs=[IN_VMEM] * 2,
        out_specs=(IN_VMEM,) * 3,
        scratch_shapes=[pltpu.VMEM((rank, rows), F32)],
        compiler_params=pltpu.CompilerParams(vmem_limit_bytes=24 << 20),
        name="project",
    )(lines, matrix)


def subtract_kernel(mean, q_pieces, p_b, matrix, new_errors, q_out, out_buf, q_buf, sems, q_sem):
    rank = p_b.shape[0]
    count, height, width = q_pieces.shape
    rows, cols = matrix.shape
    per = rank // height
    step = rows // CHUNKS
    for j in range(count // per):
        for s in range(per):
            q_buf[s * height : (s + 1) * height, j * width : (j + 1) * width] = (
                q_pieces[j * per + s].astype(F32) * mean
            )
    pltpu.make_async_copy(q_buf, q_out, q_sem).start()
    q_b = q_buf[...].astype(BF16)
    left = p_b[...].T
    for i in range(CHUNKS):
        part = pl.ds(i * step, step)
        approx = jnp.dot(left[i * step : (i + 1) * step], q_b, preferred_element_type=F32)
        out_buf[part, :] = (matrix[part, :].astype(F32) - approx).astype(BF16)
        pltpu.make_async_copy(out_buf.at[part], new_errors.at[0, part], sems.at[i]).start()
    for i in range(CHUNKS):
        part = pl.ds(i * step, step)
        pltpu.make_async_copy(out_buf.at[part], new_errors.at[0, part], sems.at[i]).wait()
    pltpu.make_async_copy(q_buf, q_out, q_sem).wait()


def subtract(q_pieces, p_b, matrix):
    rows, cols = matrix.shape
    rank = p_b.shape[0]
    count = q_pieces.shape[0]
    return pl.pallas_call(
        functools.partial(subtract_kernel, 1.0 / count),
        out_shape=(
            jax.ShapeDtypeStruct((1, rows, cols), BF16),
            jax.ShapeDtypeStruct((rank, cols), F32),
        ),
        in_specs=[IN_VMEM] * 3,
        out_specs=(IN_HBM, IN_HBM),
        scratch_shapes=[
            pltpu.VMEM((rows, cols), BF16),
            pltpu.VMEM((rank, cols), F32),
            pltpu.SemaphoreType.DMA((CHUNKS,)),
            pltpu.SemaphoreType.DMA(()),
        ],
        compiler_params=pltpu.CompilerParams(vmem_limit_bytes=24 << 20),
        name="subtract",
    )(q_pieces, p_b, matrix)


def total_kernel(pieces, copies):
    total = pieces[0].astype(F32)
    for i in range(1, pieces.shape[0]):
        total = total + pieces[i].astype(F32)
    total = total.astype(copies.dtype)
    for i in range(copies.shape[0]):
        copies[i] = total


def summed_copies(pieces, count):
    return pl.pallas_call(
        total_kernel,
        out_shape=jax.ShapeDtypeStruct((count, *pieces.shape[1:]), pieces.dtype),
        in_specs=[IN_VMEM],
        out_specs=IN_VMEM,
        compiler_params=pltpu.CompilerParams(vmem_limit_bytes=4 << 20),
        name="summed_copies",
    )(pieces)


def line_kernel(lines, copies):
    count, lanes = lines.shape
    total = lines[0:8, :]
    for i in range(8, count, 8):
        total = total + lines[i : i + 8, :]
    total = total[0:4] + total[4:8]
    total = total[0:2] + total[2:4]
    total = jnp.concatenate([total] * 4, axis=0)
    for i in range(0, count, 8):
        copies[i : i + 8, :] = total


def summed_lines(lines):
    return pl.pallas_call(
        line_kernel,
        out_shape=jax.ShapeDtypeStruct(lines.shape, F32),
        in_specs=[IN_VMEM],
        out_specs=IN_VMEM,
        compiler_params=pltpu.CompilerParams(vmem_limit_bytes=4 << 20),
        name="summed_lines",
    )(lines)


def exchanged(pieces, axis):
    return lax.all_to_all(pieces, axis, split_axis=0, concat_axis=0, tiled=True)


def exchanged_lines(lines):
    axes = ("dp", "tensor")
    return exchanged(lines.reshape(lax.axis_size(axes), -1, LANES), axes).reshape(lines.shape)


def on_device(grads, errors, basis):
    n_dp = lax.axis_size("dp")
    matrix, partial = merge(grads, errors, basis.T)
    lines = exchanged_lines(summed_lines(exchanged_lines(partial)))
    p_own, p_b, q_pieces = project(lines, matrix, n_dp)
    q_sums = exchanged(summed_copies(exchanged(q_pieces, "dp"), n_dp), "dp")
    new_errors, q_out = subtract(q_sums, p_b, matrix)
    return new_errors, p_own.T, q_out.T


def solution(mesh):
    return jax.shard_map(
        on_device,
        mesh=mesh,
        in_specs=(P("dp", None, "tensor"), P("dp", None, "tensor"), P("tensor", None)),
        out_specs=(P("dp", None, "tensor"), P("tensor", None), P("tensor", None)),
        check_vma=False,
    )
```

```python
import functools

import jax
import jax.numpy as jnp
from jax import lax
from jax.experimental import pallas as pl
from jax.experimental.pallas import tpu as pltpu
from jax.sharding import PartitionSpec as P

BF16, F32 = jnp.bfloat16, jnp.float32
HIGHEST = lax.Precision.HIGHEST
LAST_BY_LAST = (((1,), (1,)), ((), ()))
IN_VMEM = pl.BlockSpec(memory_space=pltpu.VMEM)
IN_HBM = pl.BlockSpec(memory_space=pltpu.HBM)
LANES = 128
CHUNKS = 16
BLOCK = 16
WIDTHS = (768, 768, 768, 512, 512, 256)
STARTS = tuple(sum(WIDTHS[:i]) for i in range(len(WIDTHS)))


def on_first_core():
    return lax.rem(lax.axis_index("tensor"), 2) == 0


def merge_kernel(grads, errors, basis_t, matrix, kept, sent, held, partial, grad_sems, error_sems):
    def copies(i):
        part = (slice(None), pl.ds(STARTS[i], WIDTHS[i]))
        return (
            pltpu.make_async_copy(grads.at[(0, *part)], matrix.at[part], grad_sems.at[i]),
            pltpu.make_async_copy(errors.at[(0, *part)], held.at[part], error_sems.at[i]),
        )

    for i in range(len(WIDTHS)):
        for copy in copies(i):
            copy.start()
    basis_b = basis_t[...].astype(BF16)
    half = kept.shape[1]
    first = on_first_core()
    for i in range(len(WIDTHS)):
        for copy in copies(i):
            copy.wait()
        part = slice(STARTS[i], STARTS[i] + WIDTHS[i])
        total = matrix[:, part] + held[:, part]
        matrix[:, part] = total
        product = lax.dot_general(basis_b[:, part], total, LAST_BY_LAST, preferred_element_type=F32)
        if i:
            product = partial[...] + product
        if i < len(WIDTHS) - 1:
            partial[...] = product
    kept[...] = jnp.where(first, product[:, :half], product[:, half:])
    sent[...] = jnp.where(first, product[:, half:], product[:, :half])


def merge(grads, errors, basis_t):
    rows, cols = grads.shape[1:]
    rank = basis_t.shape[0]
    return pl.pallas_call(
        merge_kernel,
        out_shape=(
            jax.ShapeDtypeStruct((rows, cols), BF16),
            jax.ShapeDtypeStruct((rank, rows // 2), F32),
            jax.ShapeDtypeStruct((rank, rows // 2), F32),
        ),
        in_specs=[IN_HBM, IN_HBM, IN_VMEM],
        out_specs=(IN_VMEM,) * 3,
        scratch_shapes=[
            pltpu.VMEM((rows, cols), BF16),
            pltpu.VMEM((rank, rows), F32),
            pltpu.SemaphoreType.DMA((len(WIDTHS),)),
            pltpu.SemaphoreType.DMA((len(WIDTHS),)),
        ],
        compiler_params=pltpu.CompilerParams(vmem_limit_bytes=44 << 20),
        name="merge",
    )(grads, errors, basis_t)


def inverse_factor(gram):
    rank = gram.shape[0]
    row = lax.broadcasted_iota(jnp.int32, (rank, LANES), 0)
    lane = lax.broadcasted_iota(jnp.int32, (rank, LANES), 1)
    work = jnp.concatenate([gram, jnp.zeros((rank, LANES - rank), F32)], axis=1)
    work = work + jnp.where(lane == row + rank, 1.0, 0.0)
    scale = jnp.zeros((rank, LANES), F32)
    for k in range(0, rank, BLOCK):
        columns = [jnp.broadcast_to(work[:, k + p : k + p + 1], (rank, LANES)) for p in range(BLOCK)]
        lines = [work[k + p : k + p + 1, :] for p in range(BLOCK)]
        scaled = []
        for p in range(BLOCK):
            pivot = columns[p][k + p : k + p + 1, :]
            inverse = 1.0 / pivot
            for q in range(p + 1, BLOCK):
                factor = columns[p][k + q : k + q + 1, :] * inverse
                lines[q] = lines[q] - factor * lines[p]
                columns[q] = columns[q] - factor * columns[p]
            scale = jnp.where(row == k + p, pivot, scale)
            work = jnp.where(row == k + p, lines[p], work)
            scaled.append(lines[p] * inverse)
        for p in range(BLOCK):
            work = work - jnp.where(row >= k + BLOCK, columns[p], 0.0) * scaled[p]
    return (work * lax.rsqrt(scale))[:, rank : 2 * rank]


def project_kernel(mine, other, matrix, p_own, p_b, q_pieces, whole):
    rank, half = mine.shape
    first = on_first_core()
    whole[:, :half] = jnp.where(first, mine[...], other[...])
    whole[:, half:] = jnp.where(first, other[...], mine[...])
    p_sum = whole[...]
    gram = lax.dot_general(p_sum, p_sum, LAST_BY_LAST, precision=HIGHEST, preferred_element_type=F32)
    inverse = inverse_factor(gram)
    own = whole[:, pl.ds(pl.multiple_of(lax.axis_index("tensor") * LANES, LANES), LANES)]
    p_own[...] = jnp.dot(inverse, own, precision=HIGHEST, preferred_element_type=F32)
    rounded = jnp.dot(inverse, p_sum, precision=HIGHEST, preferred_element_type=F32).astype(BF16)
    p_b[...] = rounded
    count, height, width = q_pieces.shape
    for j in range(count * height // rank):
        q = jnp.dot(rounded, matrix[:, j * width : (j + 1) * width], preferred_element_type=F32).astype(BF16)
        for s in range(rank // height):
            q_pieces[j * (rank // height) + s] = q[s * height : (s + 1) * height]


def project(mine, other, matrix, count):
    rank = mine.shape[0]
    rows, cols = matrix.shape
    height = 8
    width = cols * rank // (count * height)
    return pl.pallas_call(
        project_kernel,
        out_shape=(
            jax.ShapeDtypeStruct((rank, LANES), F32),
            jax.ShapeDtypeStruct((rank, rows), BF16),
            jax.ShapeDtypeStruct((count, height, width), BF16),
        ),
        in_specs=[IN_VMEM] * 3,
        out_specs=(IN_VMEM,) * 3,
        scratch_shapes=[pltpu.VMEM((rank, rows), F32)],
        compiler_params=pltpu.CompilerParams(vmem_limit_bytes=24 << 20),
        name="project",
    )(mine, other, matrix)


def subtract_kernel(mean, q_pieces, p_b, matrix, new_errors, q_out, out_buf, q_buf, sems, q_sem):
    rank = p_b.shape[0]
    count, height, width = q_pieces.shape
    rows, cols = matrix.shape
    per = rank // height
    step = rows // CHUNKS
    for j in range(count // per):
        for s in range(per):
            q_buf[s * height : (s + 1) * height, j * width : (j + 1) * width] = (
                q_pieces[j * per + s].astype(F32) * mean
            )
    pltpu.make_async_copy(q_buf, q_out, q_sem).start()
    q_b = q_buf[...].astype(BF16)
    left = p_b[...].T
    for i in range(CHUNKS):
        part = pl.ds(i * step, step)
        approx = jnp.dot(left[i * step : (i + 1) * step], q_b, preferred_element_type=F32)
        out_buf[part, :] = (matrix[part, :].astype(F32) - approx).astype(BF16)
        pltpu.make_async_copy(out_buf.at[part], new_errors.at[0, part], sems.at[i]).start()
    for i in range(CHUNKS):
        part = pl.ds(i * step, step)
        pltpu.make_async_copy(out_buf.at[part], new_errors.at[0, part], sems.at[i]).wait()
    pltpu.make_async_copy(q_buf, q_out, q_sem).wait()


def subtract(q_pieces, p_b, matrix):
    rows, cols = matrix.shape
    rank = p_b.shape[0]
    count = q_pieces.shape[0]
    return pl.pallas_call(
        functools.partial(subtract_kernel, 1.0 / count),
        out_shape=(
            jax.ShapeDtypeStruct((1, rows, cols), BF16),
            jax.ShapeDtypeStruct((rank, cols), F32),
        ),
        in_specs=[IN_VMEM] * 3,
        out_specs=(IN_HBM, IN_HBM),
        scratch_shapes=[
            pltpu.VMEM((rows, cols), BF16),
            pltpu.VMEM((rank, cols), F32),
            pltpu.SemaphoreType.DMA((CHUNKS,)),
            pltpu.SemaphoreType.DMA(()),
        ],
        compiler_params=pltpu.CompilerParams(vmem_limit_bytes=24 << 20),
        name="subtract",
    )(q_pieces, p_b, matrix)


def total_kernel(pieces, copies):
    total = pieces[0].astype(F32)
    for i in range(1, pieces.shape[0]):
        total = total + pieces[i].astype(F32)
    total = total.astype(copies.dtype)
    for i in range(copies.shape[0]):
        copies[i] = total


def summed_copies(pieces, count):
    return pl.pallas_call(
        total_kernel,
        out_shape=jax.ShapeDtypeStruct((count, *pieces.shape[1:]), pieces.dtype),
        in_specs=[IN_VMEM],
        out_specs=IN_VMEM,
        compiler_params=pltpu.CompilerParams(vmem_limit_bytes=4 << 20),
        name="summed_copies",
    )(pieces)


def added_kernel(*refs):
    terms = [ref[...] for ref in refs[:-1]]
    while len(terms) > 1:
        terms = [terms[i] + terms[i + 1] for i in range(0, len(terms), 2)]
    refs[-1][...] = terms[0]


def added(*terms):
    return pl.pallas_call(
        added_kernel,
        out_shape=jax.ShapeDtypeStruct(terms[0].shape, terms[0].dtype),
        in_specs=[IN_VMEM] * len(terms),
        out_specs=IN_VMEM,
        compiler_params=pltpu.CompilerParams(vmem_limit_bytes=4 << 20),
        name="added",
    )(*terms)


def swapped(value, axis, stride, distance):
    return lax.ppermute(value, axis, [(i, i ^ (distance * stride)) for i in range(lax.axis_size(axis))])


def summed_over_four(value, axis, stride):
    one, three, two = (swapped(value, axis, stride, distance) for distance in (1, 3, 2))
    return added(value, one, two, three)


def exchanged(pieces, axis):
    return lax.all_to_all(pieces, axis, split_axis=0, concat_axis=0, tiled=True)


def on_device(grads, errors, basis):
    matrix, kept, sent = merge(grads, errors, basis.T)
    mine = added(kept, swapped(sent, "tensor", 1, 1))
    mine = summed_over_four(mine, "tensor", 2)
    mine = summed_over_four(mine, "dp", 4)
    mine = summed_over_four(mine, "dp", 1)
    n_dp = lax.axis_size("dp")
    p_own, p_b, q_pieces = project(mine, swapped(mine, "tensor", 1, 1), matrix, n_dp)
    q_sums = exchanged(summed_copies(exchanged(q_pieces, "dp"), n_dp), "dp")
    new_errors, q_out = subtract(q_sums, p_b, matrix)
    return new_errors, p_own.T, q_out.T


def solution(mesh):
    return jax.shard_map(
        on_device,
        mesh=mesh,
        in_specs=(P("dp", None, "tensor"), P("dp", None, "tensor"), P("tensor", None)),
        out_specs=(P("dp", None, "tensor"), P("tensor", None), P("tensor", None)),
        check_vma=False,
    )
```

```python
import functools

import jax
import jax.numpy as jnp
from jax import lax
from jax.experimental import pallas as pl
from jax.experimental.pallas import tpu as pltpu
from jax.sharding import PartitionSpec as P

BF16, F32 = jnp.bfloat16, jnp.float32
HIGHEST = lax.Precision.HIGHEST
LAST_BY_LAST = (((1,), (1,)), ((), ()))
IN_VMEM = pl.BlockSpec(memory_space=pltpu.VMEM)
IN_HBM = pl.BlockSpec(memory_space=pltpu.HBM)
LANES = 128
CHUNKS = 16
BLOCK = 16
WIDTHS = (768, 768, 768, 512, 512, 256)
STARTS = tuple(sum(WIDTHS[:i]) for i in range(len(WIDTHS)))


def on_first_core():
    return lax.rem(lax.axis_index("tensor"), 2) == 0


def merge_kernel(grads, errors, basis_t, matrix, kept, sent, held, partial, grad_sems, error_sems):
    def copies(i):
        part = (slice(None), pl.ds(STARTS[i], WIDTHS[i]))
        return (
            pltpu.make_async_copy(grads.at[(0, *part)], matrix.at[part], grad_sems.at[i]),
            pltpu.make_async_copy(errors.at[(0, *part)], held.at[part], error_sems.at[i]),
        )

    for i in range(len(WIDTHS)):
        for copy in copies(i):
            copy.start()
    basis_b = basis_t[...].astype(BF16)
    half = kept.shape[1]
    first = on_first_core()
    for i in range(len(WIDTHS)):
        for copy in copies(i):
            copy.wait()
        part = slice(STARTS[i], STARTS[i] + WIDTHS[i])
        total = matrix[:, part] + held[:, part]
        matrix[:, part] = total
        product = lax.dot_general(basis_b[:, part], total, LAST_BY_LAST, preferred_element_type=F32)
        if i:
            product = partial[...] + product
        if i < len(WIDTHS) - 1:
            partial[...] = product
    kept[...] = jnp.where(first, product[:, :half], product[:, half:])
    sent[...] = jnp.where(first, product[:, half:], product[:, :half])


def merge(grads, errors, basis_t):
    rows, cols = grads.shape[1:]
    rank = basis_t.shape[0]
    return pl.pallas_call(
        merge_kernel,
        out_shape=(
            jax.ShapeDtypeStruct((rows, cols), BF16),
            jax.ShapeDtypeStruct((rank, rows // 2), F32),
            jax.ShapeDtypeStruct((rank, rows // 2), F32),
        ),
        in_specs=[IN_HBM, IN_HBM, IN_VMEM],
        out_specs=(IN_VMEM,) * 3,
        scratch_shapes=[
            pltpu.VMEM((rows, cols), BF16),
            pltpu.VMEM((rank, rows), F32),
            pltpu.SemaphoreType.DMA((len(WIDTHS),)),
            pltpu.SemaphoreType.DMA((len(WIDTHS),)),
        ],
        compiler_params=pltpu.CompilerParams(vmem_limit_bytes=44 << 20),
        name="merge",
    )(grads, errors, basis_t)


def inverse_factor(gram):
    rank = gram.shape[0]
    row = lax.broadcasted_iota(jnp.int32, (rank, LANES), 0)
    lane = lax.broadcasted_iota(jnp.int32, (rank, LANES), 1)
    work = jnp.concatenate([gram, jnp.zeros((rank, LANES - rank), F32)], axis=1)
    work = work + jnp.where(lane == row + rank, 1.0, 0.0)
    scale = jnp.zeros((rank, LANES), F32)
    for k in range(0, rank, BLOCK):
        columns = [jnp.broadcast_to(work[:, k + p : k + p + 1], (rank, LANES)) for p in range(BLOCK)]
        lines = [work[k + p : k + p + 1, :] for p in range(BLOCK)]
        scaled = []
        for p in range(BLOCK):
            pivot = columns[p][k + p : k + p + 1, :]
            inverse = 1.0 / pivot
            for q in range(p + 1, BLOCK):
                factor = columns[p][k + q : k + q + 1, :] * inverse
                lines[q] = lines[q] - factor * lines[p]
                columns[q] = columns[q] - factor * columns[p]
            scale = jnp.where(row == k + p, pivot, scale)
            work = jnp.where(row == k + p, lines[p], work)
            scaled.append(lines[p] * inverse)
        for p in range(BLOCK):
            work = work - jnp.where(row >= k + BLOCK, columns[p], 0.0) * scaled[p]
    return (work * lax.rsqrt(scale))[:, rank : 2 * rank]


def project_kernel(mine, other, matrix, p_own, p_b, q_pieces, whole):
    rank, half = mine.shape
    first = on_first_core()
    whole[:, :half] = jnp.where(first, mine[...], other[...])
    whole[:, half:] = jnp.where(first, other[...], mine[...])
    p_sum = whole[...]
    gram = lax.dot_general(p_sum, p_sum, LAST_BY_LAST, precision=HIGHEST, preferred_element_type=F32)
    inverse = inverse_factor(gram)
    own = whole[:, pl.ds(pl.multiple_of(lax.axis_index("tensor") * LANES, LANES), LANES)]
    p_own[...] = jnp.dot(inverse, own, precision=HIGHEST, preferred_element_type=F32)
    rounded = jnp.dot(inverse, p_sum, precision=HIGHEST, preferred_element_type=F32).astype(BF16)
    p_b[...] = rounded
    count, height, width = q_pieces.shape
    for j in range(count * height // rank):
        q = jnp.dot(rounded, matrix[:, j * width : (j + 1) * width], preferred_element_type=F32).astype(BF16)
        for s in range(rank // height):
            q_pieces[j * (rank // height) + s] = q[s * height : (s + 1) * height]


def project(mine, other, matrix, count):
    rank = mine.shape[0]
    rows, cols = matrix.shape
    height = 8
    width = cols * rank // (count * height)
    return pl.pallas_call(
        project_kernel,
        out_shape=(
            jax.ShapeDtypeStruct((rank, LANES), F32),
            jax.ShapeDtypeStruct((rank, rows), BF16),
            jax.ShapeDtypeStruct((count, height, width), BF16),
        ),
        in_specs=[IN_VMEM] * 3,
        out_specs=(IN_VMEM,) * 3,
        scratch_shapes=[pltpu.VMEM((rank, rows), F32)],
        compiler_params=pltpu.CompilerParams(vmem_limit_bytes=24 << 20),
        name="project",
    )(mine, other, matrix)


def subtract_kernel(mean, q_pieces, p_b, matrix, new_errors, q_out, out_buf, q_buf, sems, q_sem):
    rank = p_b.shape[0]
    count, height, width = q_pieces.shape
    rows, cols = matrix.shape
    per = rank // height
    step = rows // CHUNKS
    for j in range(count // per):
        for s in range(per):
            q_buf[s * height : (s + 1) * height, j * width : (j + 1) * width] = (
                q_pieces[j * per + s].astype(F32) * mean
            )
    pltpu.make_async_copy(q_buf, q_out, q_sem).start()
    q_b = q_buf[...].astype(BF16)
    left = p_b[...].T
    for i in range(CHUNKS):
        part = pl.ds(i * step, step)
        approx = jnp.dot(left[i * step : (i + 1) * step], q_b, preferred_element_type=F32)
        out_buf[part, :] = (matrix[part, :].astype(F32) - approx).astype(BF16)
        pltpu.make_async_copy(out_buf.at[part], new_errors.at[0, part], sems.at[i]).start()
    for i in range(CHUNKS):
        part = pl.ds(i * step, step)
        pltpu.make_async_copy(out_buf.at[part], new_errors.at[0, part], sems.at[i]).wait()
    pltpu.make_async_copy(q_buf, q_out, q_sem).wait()


def subtract(q_pieces, p_b, matrix):
    rows, cols = matrix.shape
    rank = p_b.shape[0]
    count = q_pieces.shape[0]
    return pl.pallas_call(
        functools.partial(subtract_kernel, 1.0 / count),
        out_shape=(
            jax.ShapeDtypeStruct((1, rows, cols), BF16),
            jax.ShapeDtypeStruct((rank, cols), F32),
        ),
        in_specs=[IN_VMEM] * 3,
        out_specs=(IN_HBM, IN_HBM),
        scratch_shapes=[
            pltpu.VMEM((rows, cols), BF16),
            pltpu.VMEM((rank, cols), F32),
            pltpu.SemaphoreType.DMA((CHUNKS,)),
            pltpu.SemaphoreType.DMA(()),
        ],
        compiler_params=pltpu.CompilerParams(vmem_limit_bytes=24 << 20),
        name="subtract",
    )(q_pieces, p_b, matrix)


def total_kernel(pieces, copies):
    total = pieces[0].astype(F32)
    for i in range(1, pieces.shape[0]):
        total = total + pieces[i].astype(F32)
    total = total.astype(copies.dtype)
    for i in range(copies.shape[0]):
        copies[i] = total


def summed_copies(pieces, count):
    return pl.pallas_call(
        total_kernel,
        out_shape=jax.ShapeDtypeStruct((count, *pieces.shape[1:]), pieces.dtype),
        in_specs=[IN_VMEM],
        out_specs=IN_VMEM,
        compiler_params=pltpu.CompilerParams(vmem_limit_bytes=4 << 20),
        name="summed_copies",
    )(pieces)


def added_kernel(*refs):
    terms = [ref[...] for ref in refs[:-1]]
    while len(terms) > 1:
        terms = [terms[i] + terms[i + 1] for i in range(0, len(terms), 2)]
    refs[-1][...] = terms[0]


def added(*terms):
    return pl.pallas_call(
        added_kernel,
        out_shape=jax.ShapeDtypeStruct(terms[0].shape, terms[0].dtype),
        in_specs=[IN_VMEM] * len(terms),
        out_specs=IN_VMEM,
        compiler_params=pltpu.CompilerParams(vmem_limit_bytes=4 << 20),
        name="added",
    )(*terms)


def swapped(value, axis, stride, distance):
    return lax.ppermute(value, axis, [(i, i ^ (distance * stride)) for i in range(lax.axis_size(axis))])


def summed_over_four(value, axis, stride):
    one, three, two = (swapped(value, axis, stride, distance) for distance in (1, 3, 2))
    return added(value, one, three, two)


def exchanged(pieces, axis):
    return lax.all_to_all(pieces, axis, split_axis=0, concat_axis=0, tiled=True)


def on_device(grads, errors, basis):
    matrix, kept, sent = merge(grads, errors, basis.T)
    mine = added(kept, swapped(sent, "tensor", 1, 1))
    mine = summed_over_four(mine, "tensor", 2)
    mine = summed_over_four(mine, "dp", 4)
    mine = summed_over_four(mine, "dp", 1)
    n_dp = lax.axis_size("dp")
    p_own, p_b, q_pieces = project(mine, swapped(mine, "tensor", 1, 1), matrix, n_dp)
    q_sums = exchanged(summed_copies(exchanged(q_pieces, "dp"), n_dp), "dp")
    new_errors, q_out = subtract(q_sums, p_b, matrix)
    return new_errors, p_own.T, q_out.T


def solution(mesh):
    return jax.shard_map(
        on_device,
        mesh=mesh,
        in_specs=(P("dp", None, "tensor"), P("dp", None, "tensor"), P("tensor", None)),
        out_specs=(P("dp", None, "tensor"), P("tensor", None), P("tensor", None)),
        check_vma=False,
    )
```

```python
import functools

import jax
import jax.numpy as jnp
from jax import lax
from jax.experimental import pallas as pl
from jax.experimental.pallas import tpu as pltpu
from jax.sharding import PartitionSpec as P

BF16, F32 = jnp.bfloat16, jnp.float32
HIGHEST = lax.Precision.HIGHEST
LAST_BY_LAST = (((1,), (1,)), ((), ()))
IN_VMEM = pl.BlockSpec(memory_space=pltpu.VMEM)
IN_HBM = pl.BlockSpec(memory_space=pltpu.HBM)
LANES = 128
CHUNKS = 4
BLOCK = 16
RING = 4
FAR_FIRST = (2, 3, 1, 0)
WIDTHS = (768, 768, 768, 512, 512, 256)
STARTS = tuple(sum(WIDTHS[:i]) for i in range(len(WIDTHS)))


def on_first_core():
    return lax.rem(lax.axis_index("tensor"), 2) == 0


def merge_kernel(grads, errors, basis_t, matrix, kept, sent, held, partial, grad_sems, error_sems):
    def copies(i):
        part = (slice(None), pl.ds(STARTS[i], WIDTHS[i]))
        return (
            pltpu.make_async_copy(grads.at[(0, *part)], matrix.at[part], grad_sems.at[i]),
            pltpu.make_async_copy(errors.at[(0, *part)], held.at[part], error_sems.at[i]),
        )

    for i in range(len(WIDTHS)):
        for copy in copies(i):
            copy.start()
    basis_b = basis_t[...].astype(BF16)
    half = kept.shape[1]
    first = on_first_core()
    for i in range(len(WIDTHS)):
        for copy in copies(i):
            copy.wait()
        part = slice(STARTS[i], STARTS[i] + WIDTHS[i])
        total = matrix[:, part] + held[:, part]
        matrix[:, part] = total
        product = lax.dot_general(basis_b[:, part], total, LAST_BY_LAST, preferred_element_type=F32)
        if i:
            product = partial[...] + product
        if i < len(WIDTHS) - 1:
            partial[...] = product
    kept[...] = jnp.where(first, product[:, :half], product[:, half:])
    sent[...] = jnp.where(first, product[:, half:], product[:, :half])


def merge(grads, errors, basis_t):
    rows, cols = grads.shape[1:]
    rank = basis_t.shape[0]
    return pl.pallas_call(
        merge_kernel,
        out_shape=(
            jax.ShapeDtypeStruct((rows, cols), BF16),
            jax.ShapeDtypeStruct((rank, rows // 2), F32),
            jax.ShapeDtypeStruct((rank, rows // 2), F32),
        ),
        in_specs=[IN_HBM, IN_HBM, IN_VMEM],
        out_specs=(IN_VMEM,) * 3,
        scratch_shapes=[
            pltpu.VMEM((rows, cols), BF16),
            pltpu.VMEM((rank, rows), F32),
            pltpu.SemaphoreType.DMA((len(WIDTHS),)),
            pltpu.SemaphoreType.DMA((len(WIDTHS),)),
        ],
        compiler_params=pltpu.CompilerParams(vmem_limit_bytes=44 << 20),
        name="merge",
    )(grads, errors, basis_t)


def inverse_factor(gram):
    rank = gram.shape[0]
    row = lax.broadcasted_iota(jnp.int32, (rank, LANES), 0)
    lane = lax.broadcasted_iota(jnp.int32, (rank, LANES), 1)
    work = jnp.concatenate([gram, jnp.zeros((rank, LANES - rank), F32)], axis=1)
    work = work + jnp.where(lane == row + rank, 1.0, 0.0)
    scale = jnp.zeros((rank, LANES), F32)
    for k in range(0, rank, BLOCK):
        columns = [jnp.broadcast_to(work[:, k + p : k + p + 1], (rank, LANES)) for p in range(BLOCK)]
        lines = [work[k + p : k + p + 1, :] for p in range(BLOCK)]
        scaled = []
        for p in range(BLOCK):
            pivot = columns[p][k + p : k + p + 1, :]
            inverse = 1.0 / pivot
            for q in range(p + 1, BLOCK):
                factor = columns[p][k + q : k + q + 1, :] * inverse
                lines[q] = lines[q] - factor * lines[p]
                columns[q] = columns[q] - factor * columns[p]
            scale = jnp.where(row == k + p, pivot, scale)
            work = jnp.where(row == k + p, lines[p], work)
            scaled.append(lines[p] * inverse)
        for p in range(BLOCK):
            work = work - jnp.where(row >= k + BLOCK, columns[p], 0.0) * scaled[p]
    return (work * lax.rsqrt(scale))[:, rank : 2 * rank]


def project_kernel(mine, other, matrix, p_own, p_b, *refs):
    *q_parts, whole = refs
    rank, half = mine.shape
    first = on_first_core()
    whole[:, :half] = jnp.where(first, mine[...], other[...])
    whole[:, half:] = jnp.where(first, other[...], mine[...])
    p_sum = whole[...]
    gram = lax.dot_general(p_sum, p_sum, LAST_BY_LAST, precision=HIGHEST, preferred_element_type=F32)
    inverse = inverse_factor(gram)
    own = whole[:, pl.ds(pl.multiple_of(lax.axis_index("tensor") * LANES, LANES), LANES)]
    p_own[...] = jnp.dot(inverse, own, precision=HIGHEST, preferred_element_type=F32)
    rounded = jnp.dot(inverse, p_sum, precision=HIGHEST, preferred_element_type=F32).astype(BF16)
    p_b[...] = rounded
    width = q_parts[0].shape[1]
    position = lax.rem(lax.axis_index("dp"), RING)
    for distance in FAR_FIRST:
        cols = pl.ds(pl.multiple_of((position ^ distance) * width, LANES), width)
        product = jnp.dot(rounded, matrix[:, cols], preferred_element_type=F32)
        q_parts[distance][...] = product.astype(BF16)


def project(mine, other, matrix):
    rank = mine.shape[0]
    rows, cols = matrix.shape
    return pl.pallas_call(
        project_kernel,
        out_shape=(
            jax.ShapeDtypeStruct((rank, LANES), F32),
            jax.ShapeDtypeStruct((rank, rows), BF16),
            *[jax.ShapeDtypeStruct((rank, cols // RING), BF16)] * RING,
        ),
        in_specs=[IN_VMEM] * 3,
        out_specs=(IN_VMEM,) * (2 + RING),
        scratch_shapes=[pltpu.VMEM((rank, rows), F32)],
        compiler_params=pltpu.CompilerParams(vmem_limit_bytes=24 << 20),
        name="project",
    )(mine, other, matrix)


def subtract_kernel(mean, distance, q_part, p_b, matrix, *refs):
    new_errors, q_out, out_buf, q_buf, sems, q_sem = refs[-6:]
    width = q_part.shape[1]
    rows = matrix.shape[0]
    step = rows // CHUNKS
    position = lax.rem(lax.axis_index("dp"), RING)
    cols = pl.ds(pl.multiple_of((position ^ distance) * width, LANES), width)
    q_buf[...] = q_part[...].astype(F32) * mean
    q_copy = pltpu.make_async_copy(q_buf, q_out.at[:, cols], q_sem)
    q_copy.start()
    q_b = q_buf[...].astype(BF16)
    left = p_b[...].T
    copies = []
    for i in range(CHUNKS):
        part = pl.ds(i * step, step)
        approx = jnp.dot(left[i * step : (i + 1) * step], q_b, preferred_element_type=F32)
        out_buf[part, :] = (matrix[part, cols].astype(F32) - approx).astype(BF16)
        copies.append(pltpu.make_async_copy(out_buf.at[part], new_errors.at[0, part, cols], sems.at[i]))
        copies[-1].start()
    for copy in copies:
        copy.wait()
    q_copy.wait()


def subtract(q_part, p_b, matrix, mean, distance, earlier):
    rows, cols = matrix.shape
    rank, width = q_part.shape
    return pl.pallas_call(
        functools.partial(subtract_kernel, mean, distance),
        out_shape=(
            jax.ShapeDtypeStruct((1, rows, cols), BF16),
            jax.ShapeDtypeStruct((rank, cols), F32),
        ),
        in_specs=[IN_VMEM] * 3 + [IN_HBM] * len(earlier),
        out_specs=(IN_HBM, IN_HBM),
        scratch_shapes=[
            pltpu.VMEM((rows, width), BF16),
            pltpu.VMEM((rank, width), F32),
            pltpu.SemaphoreType.DMA((CHUNKS,)),
            pltpu.SemaphoreType.DMA(()),
        ],
        input_output_aliases={3: 0, 4: 1} if earlier else {},
        compiler_params=pltpu.CompilerParams(vmem_limit_bytes=12 << 20),
        cost_estimate=pl.CostEstimate(flops=2 * rows * width * rank, bytes_accessed=2 * rows * width, transcendentals=0),
        name="subtract",
    )(q_part, p_b, matrix, *earlier)


def added_kernel(*refs):
    terms = [ref[...].astype(F32) for ref in refs[:-1]]
    while len(terms) > 1:
        terms = [terms[i] + terms[i + 1] for i in range(0, len(terms), 2)]
    refs[-1][...] = terms[0].astype(refs[-1].dtype)


def added(*terms):
    return pl.pallas_call(
        added_kernel,
        out_shape=jax.ShapeDtypeStruct(terms[0].shape, terms[0].dtype),
        in_specs=[IN_VMEM] * len(terms),
        out_specs=IN_VMEM,
        compiler_params=pltpu.CompilerParams(vmem_limit_bytes=4 << 20),
        name="added",
    )(*terms)


def swapped(value, axis, stride, distance):
    return lax.ppermute(value, axis, [(i, i ^ (distance * stride)) for i in range(lax.axis_size(axis))])


def summed_over_four(value, axis, stride):
    one, three, two = (swapped(value, axis, stride, distance) for distance in (1, 3, 2))
    return added(two, three, one, value)


def on_device(grads, errors, basis):
    matrix, kept, sent = merge(grads, errors, basis.T)
    mine = added(kept, swapped(sent, "tensor", 1, 1))
    mine = summed_over_four(mine, "tensor", 2)
    mine = summed_over_four(mine, "dp", 4)
    mine = summed_over_four(mine, "dp", 1)
    p_own, p_b, *q_parts = project(mine, swapped(mine, "tensor", 1, 1), matrix)
    one, three, two = (swapped(q_parts[distance], "dp", 1, distance) for distance in (1, 3, 2))
    q_sum = summed_over_four(added(two, three, one, q_parts[0]), "dp", 4)
    mean, earlier = 1.0 / lax.axis_size("dp"), ()
    for distance in (0, 2, 1, 3):
        q_part = swapped(q_sum, "dp", 1, distance) if distance else q_sum
        earlier = subtract(q_part, p_b, matrix, mean, distance, earlier)
    new_errors, q_out = earlier
    return new_errors, p_own.T, q_out.T


def solution(mesh):
    return jax.shard_map(
        on_device,
        mesh=mesh,
        in_specs=(P("dp", None, "tensor"), P("dp", None, "tensor"), P("tensor", None)),
        out_specs=(P("dp", None, "tensor"), P("tensor", None), P("tensor", None)),
        check_vma=False,
    )
```

```python
import functools

import jax
import jax.numpy as jnp
from jax import lax
from jax.experimental import pallas as pl
from jax.experimental.pallas import tpu as pltpu
from jax.sharding import PartitionSpec as P

BF16, F32 = jnp.bfloat16, jnp.float32
HIGHEST = lax.Precision.HIGHEST
LAST_BY_LAST = (((1,), (1,)), ((), ()))
IN_VMEM = pl.BlockSpec(memory_space=pltpu.VMEM)
IN_HBM = pl.BlockSpec(memory_space=pltpu.HBM)
LANES = 128
CHUNKS = 8
BLOCK = 16
RING = 4
FAR_FIRST = (2, 3, 1, 0)
WIDTHS = (768, 768, 768, 512, 512, 256)
STARTS = tuple(sum(WIDTHS[:i]) for i in range(len(WIDTHS)))


def on_first_core():
    return lax.rem(lax.axis_index("tensor"), 2) == 0


def merge_kernel(grads, errors, basis_t, matrix, kept, sent, held, partial, grad_sems, error_sems):
    def copies(i):
        part = (slice(None), pl.ds(STARTS[i], WIDTHS[i]))
        return (
            pltpu.make_async_copy(grads.at[(0, *part)], matrix.at[part], grad_sems.at[i]),
            pltpu.make_async_copy(errors.at[(0, *part)], held.at[part], error_sems.at[i]),
        )

    for i in range(len(WIDTHS)):
        for copy in copies(i):
            copy.start()
    basis_b = basis_t[...].astype(BF16)
    half = kept.shape[1]
    first = on_first_core()
    for i in range(len(WIDTHS)):
        for copy in copies(i):
            copy.wait()
        part = slice(STARTS[i], STARTS[i] + WIDTHS[i])
        total = matrix[:, part] + held[:, part]
        matrix[:, part] = total
        product = lax.dot_general(basis_b[:, part], total, LAST_BY_LAST, preferred_element_type=F32)
        if i:
            product = partial[...] + product
        if i < len(WIDTHS) - 1:
            partial[...] = product
    kept[...] = jnp.where(first, product[:, :half], product[:, half:])
    sent[...] = jnp.where(first, product[:, half:], product[:, :half])


def merge(grads, errors, basis_t):
    rows, cols = grads.shape[1:]
    rank = basis_t.shape[0]
    return pl.pallas_call(
        merge_kernel,
        out_shape=(
            jax.ShapeDtypeStruct((rows, cols), BF16),
            jax.ShapeDtypeStruct((rank, rows // 2), F32),
            jax.ShapeDtypeStruct((rank, rows // 2), F32),
        ),
        in_specs=[IN_HBM, IN_HBM, IN_VMEM],
        out_specs=(IN_VMEM,) * 3,
        scratch_shapes=[
            pltpu.VMEM((rows, cols), BF16),
            pltpu.VMEM((rank, rows), F32),
            pltpu.SemaphoreType.DMA((len(WIDTHS),)),
            pltpu.SemaphoreType.DMA((len(WIDTHS),)),
        ],
        compiler_params=pltpu.CompilerParams(vmem_limit_bytes=44 << 20),
        name="merge",
    )(grads, errors, basis_t)


def inverse_factor(gram):
    rank = gram.shape[0]
    row = lax.broadcasted_iota(jnp.int32, (rank, LANES), 0)
    lane = lax.broadcasted_iota(jnp.int32, (rank, LANES), 1)
    work = jnp.concatenate([gram, jnp.zeros((rank, LANES - rank), F32)], axis=1)
    work = work + jnp.where(lane == row + rank, 1.0, 0.0)
    scale = jnp.zeros((rank, LANES), F32)
    for k in range(0, rank, BLOCK):
        columns = [jnp.broadcast_to(work[:, k + p : k + p + 1], (rank, LANES)) for p in range(BLOCK)]
        lines = [work[k + p : k + p + 1, :] for p in range(BLOCK)]
        scaled = []
        for p in range(BLOCK):
            pivot = columns[p][k + p : k + p + 1, :]
            inverse = 1.0 / pivot
            for q in range(p + 1, BLOCK):
                factor = columns[p][k + q : k + q + 1, :] * inverse
                lines[q] = lines[q] - factor * lines[p]
                columns[q] = columns[q] - factor * columns[p]
            scale = jnp.where(row == k + p, pivot, scale)
            work = jnp.where(row == k + p, lines[p], work)
            scaled.append(lines[p] * inverse)
        for p in range(BLOCK):
            work = work - jnp.where(row >= k + BLOCK, columns[p], 0.0) * scaled[p]
    return (work * lax.rsqrt(scale))[:, rank : 2 * rank]


def project_kernel(mine, other, matrix, p_own, p_b, *refs):
    *q_parts, whole = refs
    rank, half = mine.shape
    first = on_first_core()
    whole[:, :half] = jnp.where(first, mine[...], other[...])
    whole[:, half:] = jnp.where(first, other[...], mine[...])
    p_sum = whole[...]
    gram = lax.dot_general(p_sum, p_sum, LAST_BY_LAST, precision=HIGHEST, preferred_element_type=F32)
    inverse = inverse_factor(gram)
    own = whole[:, pl.ds(pl.multiple_of(lax.axis_index("tensor") * LANES, LANES), LANES)]
    p_own[...] = jnp.dot(inverse, own, precision=HIGHEST, preferred_element_type=F32)
    rounded = jnp.dot(inverse, p_sum, precision=HIGHEST, preferred_element_type=F32).astype(BF16)
    p_b[...] = rounded
    width = q_parts[0].shape[1]
    position = lax.rem(lax.axis_index("dp"), RING)
    for distance in FAR_FIRST:
        cols = pl.ds(pl.multiple_of((position ^ distance) * width, LANES), width)
        product = jnp.dot(rounded, matrix[:, cols], preferred_element_type=F32)
        q_parts[distance][...] = product.astype(BF16)


def project(mine, other, matrix):
    rank = mine.shape[0]
    rows, cols = matrix.shape
    return pl.pallas_call(
        project_kernel,
        out_shape=(
            jax.ShapeDtypeStruct((rank, LANES), F32),
            jax.ShapeDtypeStruct((rank, rows), BF16),
            *[jax.ShapeDtypeStruct((rank, cols // RING), BF16)] * RING,
        ),
        in_specs=[IN_VMEM] * 3,
        out_specs=(IN_VMEM,) * (2 + RING),
        scratch_shapes=[pltpu.VMEM((rank, rows), F32)],
        compiler_params=pltpu.CompilerParams(vmem_limit_bytes=24 << 20),
        name="project",
    )(mine, other, matrix)


def subtract_kernel(mean, distances, *refs):
    q_parts, (p_b, matrix) = refs[: len(distances)], refs[len(distances) : len(distances) + 2]
    new_errors, q_out, out_buf, q_buf, sems, q_sems = refs[-6:]
    width = q_parts[0].shape[1]
    rows = matrix.shape[0]
    step = rows // CHUNKS
    position = lax.rem(lax.axis_index("dp"), RING)
    left = p_b[...].T
    copies = []
    for n, distance in enumerate(distances):
        cols = pl.ds(pl.multiple_of((position ^ distance) * width, LANES), width)
        q_buf[n] = q_parts[n][...].astype(F32) * mean
        copies.append(pltpu.make_async_copy(q_buf.at[n], q_out.at[:, cols], q_sems.at[n]))
        copies[-1].start()
        q_b = q_buf[n].astype(BF16)
        for i in range(CHUNKS):
            part = pl.ds(i * step, step)
            approx = jnp.dot(left[i * step : (i + 1) * step], q_b, preferred_element_type=F32)
            out_buf[n, part, :] = (matrix[part, cols].astype(F32) - approx).astype(BF16)
            copies.append(
                pltpu.make_async_copy(out_buf.at[n, part], new_errors.at[0, part, cols], sems.at[n, i])
            )
            copies[-1].start()
    for copy in copies:
        copy.wait()


def subtract(q_parts, p_b, matrix, mean, distances, earlier):
    rows, cols = matrix.shape
    rank, width = q_parts[0].shape
    count = len(q_parts)
    size = count * rows * width
    return pl.pallas_call(
        functools.partial(subtract_kernel, mean, distances),
        out_shape=(
            jax.ShapeDtypeStruct((1, rows, cols), BF16),
            jax.ShapeDtypeStruct((rank, cols), F32),
        ),
        in_specs=[IN_VMEM] * (count + 2) + [IN_HBM] * len(earlier),
        out_specs=(IN_HBM, IN_HBM),
        scratch_shapes=[
            pltpu.VMEM((count, rows, width), BF16),
            pltpu.VMEM((count, rank, width), F32),
            pltpu.SemaphoreType.DMA((count, CHUNKS)),
            pltpu.SemaphoreType.DMA((count,)),
        ],
        input_output_aliases={count + 2: 0, count + 3: 1} if earlier else {},
        compiler_params=pltpu.CompilerParams(vmem_limit_bytes=12 << 20),
        cost_estimate=pl.CostEstimate(flops=2 * size * rank, bytes_accessed=2 * size, transcendentals=0),
        name="subtract",
    )(*q_parts, p_b, matrix, *earlier)


def added_kernel(*refs):
    terms = [ref[...].astype(F32) for ref in refs[:-1]]
    while len(terms) > 1:
        terms = [terms[i] + terms[i + 1] for i in range(0, len(terms), 2)]
    refs[-1][...] = terms[0].astype(refs[-1].dtype)


def added(*terms):
    return pl.pallas_call(
        added_kernel,
        out_shape=jax.ShapeDtypeStruct(terms[0].shape, terms[0].dtype),
        in_specs=[IN_VMEM] * len(terms),
        out_specs=IN_VMEM,
        compiler_params=pltpu.CompilerParams(vmem_limit_bytes=4 << 20),
        name="added",
    )(*terms)


def swapped(value, axis, stride, distance):
    return lax.ppermute(value, axis, [(i, i ^ (distance * stride)) for i in range(lax.axis_size(axis))])


def summed_over_four(value, axis, stride):
    one, three, two = (swapped(value, axis, stride, distance) for distance in (1, 3, 2))
    return added(two, three, one, value)


def on_device(grads, errors, basis):
    matrix, kept, sent = merge(grads, errors, basis.T)
    mine = added(kept, swapped(sent, "tensor", 1, 1))
    mine = summed_over_four(mine, "tensor", 2)
    mine = summed_over_four(mine, "dp", 4)
    mine = summed_over_four(mine, "dp", 1)
    p_own, p_b, *q_parts = project(mine, swapped(mine, "tensor", 1, 1), matrix)
    one, three, two = (swapped(q_parts[distance], "dp", 1, distance) for distance in (1, 3, 2))
    q_sum = summed_over_four(added(two, three, one, q_parts[0]), "dp", 4)
    mean, earlier = 1.0 / lax.axis_size("dp"), ()
    for distances in ((0,), (2,), (3, 1)):
        q_now = [swapped(q_sum, "dp", 1, distance) if distance else q_sum for distance in distances]
        earlier = subtract(q_now, p_b, matrix, mean, distances, earlier)
    new_errors, q_out = earlier
    return new_errors, p_own.T, q_out.T


def solution(mesh):
    return jax.shard_map(
        on_device,
        mesh=mesh,
        in_specs=(P("dp", None, "tensor"), P("dp", None, "tensor"), P("tensor", None)),
        out_specs=(P("dp", None, "tensor"), P("tensor", None), P("tensor", None)),
        check_vma=False,
    )
```

```python
import functools

import jax
import jax.numpy as jnp
from jax import lax
from jax.experimental import pallas as pl
from jax.experimental.pallas import tpu as pltpu
from jax.sharding import PartitionSpec as P

BF16, F32 = jnp.bfloat16, jnp.float32
HIGHEST = lax.Precision.HIGHEST
LAST_BY_LAST = (((1,), (1,)), ((), ()))
IN_VMEM = pl.BlockSpec(memory_space=pltpu.VMEM)
IN_HBM = pl.BlockSpec(memory_space=pltpu.HBM)
LANES = 128
CHUNKS = 8
BLOCK = 16
RING = 4
FAR_FIRST = (2, 3, 1, 0)
WIDTHS = (768, 768, 768, 512, 512, 256)
STARTS = tuple(sum(WIDTHS[:i]) for i in range(len(WIDTHS)))


def on_first_core():
    return lax.rem(lax.axis_index("tensor"), 2) == 0


def merge_kernel(grads, errors, basis_t, matrix, kept, sent, held, partial, grad_sems, error_sems):
    def copies(i):
        part = (slice(None), pl.ds(STARTS[i], WIDTHS[i]))
        return (
            pltpu.make_async_copy(grads.at[(0, *part)], matrix.at[part], grad_sems.at[i]),
            pltpu.make_async_copy(errors.at[(0, *part)], held.at[part], error_sems.at[i]),
        )

    for i in range(len(WIDTHS)):
        for copy in copies(i):
            copy.start()
    basis_b = basis_t[...].astype(BF16)
    half = kept.shape[1]
    first = on_first_core()
    for i in range(len(WIDTHS)):
        for copy in copies(i):
            copy.wait()
        part = slice(STARTS[i], STARTS[i] + WIDTHS[i])
        total = matrix[:, part] + held[:, part]
        matrix[:, part] = total
        product = lax.dot_general(basis_b[:, part], total, LAST_BY_LAST, preferred_element_type=F32)
        if i:
            product = partial[...] + product
        if i < len(WIDTHS) - 1:
            partial[...] = product
    kept[...] = jnp.where(first, product[:, :half], product[:, half:])
    sent[...] = jnp.where(first, product[:, half:], product[:, :half])


def merge(grads, errors, basis_t):
    rows, cols = grads.shape[1:]
    rank = basis_t.shape[0]
    return pl.pallas_call(
        merge_kernel,
        out_shape=(
            jax.ShapeDtypeStruct((rows, cols), BF16),
            jax.ShapeDtypeStruct((rank, rows // 2), F32),
            jax.ShapeDtypeStruct((rank, rows // 2), F32),
        ),
        in_specs=[IN_HBM, IN_HBM, IN_VMEM],
        out_specs=(IN_VMEM,) * 3,
        scratch_shapes=[
            pltpu.VMEM((rows, cols), BF16),
            pltpu.VMEM((rank, rows), F32),
            pltpu.SemaphoreType.DMA((len(WIDTHS),)),
            pltpu.SemaphoreType.DMA((len(WIDTHS),)),
        ],
        compiler_params=pltpu.CompilerParams(vmem_limit_bytes=44 << 20),
        name="merge",
    )(grads, errors, basis_t)


def inverse_factor(gram):
    rank = gram.shape[0]
    row = lax.broadcasted_iota(jnp.int32, (rank, LANES), 0)
    lane = lax.broadcasted_iota(jnp.int32, (rank, LANES), 1)
    work = jnp.concatenate([gram, jnp.zeros((rank, LANES - rank), F32)], axis=1)
    work = work + jnp.where(lane == row + rank, 1.0, 0.0)
    scale = jnp.zeros((rank, LANES), F32)
    for k in range(0, rank, BLOCK):
        columns = [jnp.broadcast_to(work[:, k + p : k + p + 1], (rank, LANES)) for p in range(BLOCK)]
        lines = [work[k + p : k + p + 1, :] for p in range(BLOCK)]
        scaled = []
        for p in range(BLOCK):
            pivot = columns[p][k + p : k + p + 1, :]
            inverse = 1.0 / pivot
            for q in range(p + 1, BLOCK):
                factor = columns[p][k + q : k + q + 1, :] * inverse
                lines[q] = lines[q] - factor * lines[p]
                columns[q] = columns[q] - factor * columns[p]
            scale = jnp.where(row == k + p, pivot, scale)
            work = jnp.where(row == k + p, lines[p], work)
            scaled.append(lines[p] * inverse)
        for p in range(BLOCK):
            work = work - jnp.where(row >= k + BLOCK, columns[p], 0.0) * scaled[p]
    return (work * lax.rsqrt(scale))[:, rank : 2 * rank]


def project_kernel(mine, other, matrix, p_own, p_b, *refs):
    *q_parts, whole = refs
    rank, half = mine.shape
    first = on_first_core()
    whole[:, :half] = jnp.where(first, mine[...], other[...])
    whole[:, half:] = jnp.where(first, other[...], mine[...])
    p_sum = whole[...]
    gram = lax.dot_general(p_sum, p_sum, LAST_BY_LAST, precision=HIGHEST, preferred_element_type=F32)
    inverse = inverse_factor(gram)
    own = whole[:, pl.ds(pl.multiple_of(lax.axis_index("tensor") * LANES, LANES), LANES)]
    p_own[...] = jnp.dot(inverse, own, precision=HIGHEST, preferred_element_type=F32)
    rounded = jnp.dot(inverse, p_sum, precision=HIGHEST, preferred_element_type=F32).astype(BF16)
    p_b[...] = rounded
    width = q_parts[0].shape[1]
    position = lax.div(lax.axis_index("dp"), RING)
    for distance in FAR_FIRST:
        cols = pl.ds(pl.multiple_of((position ^ distance) * width, LANES), width)
        product = jnp.dot(rounded, matrix[:, cols], preferred_element_type=F32)
        q_parts[distance][...] = product.astype(BF16)


def project(mine, other, matrix):
    rank = mine.shape[0]
    rows, cols = matrix.shape
    return pl.pallas_call(
        project_kernel,
        out_shape=(
            jax.ShapeDtypeStruct((rank, LANES), F32),
            jax.ShapeDtypeStruct((rank, rows), BF16),
            *[jax.ShapeDtypeStruct((rank, cols // RING), BF16)] * RING,
        ),
        in_specs=[IN_VMEM] * 3,
        out_specs=(IN_VMEM,) * (2 + RING),
        scratch_shapes=[pltpu.VMEM((rank, rows), F32)],
        compiler_params=pltpu.CompilerParams(vmem_limit_bytes=24 << 20),
        name="project",
    )(mine, other, matrix)


def subtract_kernel(mean, distances, *refs):
    q_parts, (p_b, matrix) = refs[: len(distances)], refs[len(distances) : len(distances) + 2]
    new_errors, q_out, out_buf, q_buf, sems, q_sems = refs[-6:]
    width = q_parts[0].shape[1]
    rows = matrix.shape[0]
    step = rows // CHUNKS
    position = lax.div(lax.axis_index("dp"), RING)
    left = p_b[...].T
    copies = []
    for n, distance in enumerate(distances):
        cols = pl.ds(pl.multiple_of((position ^ distance) * width, LANES), width)
        q_buf[n] = q_parts[n][...].astype(F32) * mean
        copies.append(pltpu.make_async_copy(q_buf.at[n], q_out.at[:, cols], q_sems.at[n]))
        copies[-1].start()
        q_b = q_buf[n].astype(BF16)
        for i in range(CHUNKS):
            part = pl.ds(i * step, step)
            approx = jnp.dot(left[i * step : (i + 1) * step], q_b, preferred_element_type=F32)
            out_buf[n, part, :] = (matrix[part, cols].astype(F32) - approx).astype(BF16)
            copies.append(
                pltpu.make_async_copy(out_buf.at[n, part], new_errors.at[0, part, cols], sems.at[n, i])
            )
            copies[-1].start()
    for copy in copies:
        copy.wait()


def subtract(q_parts, p_b, matrix, mean, distances, earlier):
    rows, cols = matrix.shape
    rank, width = q_parts[0].shape
    count = len(q_parts)
    size = count * rows * width
    return pl.pallas_call(
        functools.partial(subtract_kernel, mean, distances),
        out_shape=(
            jax.ShapeDtypeStruct((1, rows, cols), BF16),
            jax.ShapeDtypeStruct((rank, cols), F32),
        ),
        in_specs=[IN_VMEM] * (count + 2) + [IN_HBM] * len(earlier),
        out_specs=(IN_HBM, IN_HBM),
        scratch_shapes=[
            pltpu.VMEM((count, rows, width), BF16),
            pltpu.VMEM((count, rank, width), F32),
            pltpu.SemaphoreType.DMA((count, CHUNKS)),
            pltpu.SemaphoreType.DMA((count,)),
        ],
        input_output_aliases={count + 2: 0, count + 3: 1} if earlier else {},
        compiler_params=pltpu.CompilerParams(vmem_limit_bytes=12 << 20),
        cost_estimate=pl.CostEstimate(flops=2 * size * rank, bytes_accessed=2 * size, transcendentals=0),
        name="subtract",
    )(*q_parts, p_b, matrix, *earlier)


def added_kernel(*refs):
    terms = [ref[...].astype(F32) for ref in refs[:-1]]
    while len(terms) > 1:
        terms = [terms[i] + terms[i + 1] for i in range(0, len(terms), 2)]
    refs[-1][...] = terms[0].astype(refs[-1].dtype)


def added(*terms):
    return pl.pallas_call(
        added_kernel,
        out_shape=jax.ShapeDtypeStruct(terms[0].shape, terms[0].dtype),
        in_specs=[IN_VMEM] * len(terms),
        out_specs=IN_VMEM,
        compiler_params=pltpu.CompilerParams(vmem_limit_bytes=4 << 20),
        name="added",
    )(*terms)


def swapped(value, axis, stride, distance):
    return lax.ppermute(value, axis, [(i, i ^ (distance * stride)) for i in range(lax.axis_size(axis))])


def summed_over_four(value, axis, stride):
    one, three, two = (swapped(value, axis, stride, distance) for distance in (1, 3, 2))
    return added(two, three, one, value)


def on_device(grads, errors, basis):
    matrix, kept, sent = merge(grads, errors, basis.T)
    mine = added(kept, swapped(sent, "tensor", 1, 1))
    mine = summed_over_four(mine, "tensor", 2)
    mine = summed_over_four(mine, "dp", 4)
    mine = summed_over_four(mine, "dp", 1)
    p_own, p_b, *q_parts = project(mine, swapped(mine, "tensor", 1, 1), matrix)
    one, three, two = (swapped(q_parts[distance], "dp", RING, distance) for distance in (1, 3, 2))
    q_sum = summed_over_four(added(two, three, one, q_parts[0]), "dp", 1)
    mean, earlier = 1.0 / lax.axis_size("dp"), ()
    for distances in ((0,), (2,), (3, 1)):
        q_now = [swapped(q_sum, "dp", RING, distance) if distance else q_sum for distance in distances]
        earlier = subtract(q_now, p_b, matrix, mean, distances, earlier)
    new_errors, q_out = earlier
    return new_errors, p_own.T, q_out.T


def solution(mesh):
    return jax.shard_map(
        on_device,
        mesh=mesh,
        in_specs=(P("dp", None, "tensor"), P("dp", None, "tensor"), P("tensor", None)),
        out_specs=(P("dp", None, "tensor"), P("tensor", None), P("tensor", None)),
        check_vma=False,
    )
```

```python
import functools

import jax
import jax.numpy as jnp
from jax import lax
from jax.experimental import pallas as pl
from jax.experimental.pallas import tpu as pltpu
from jax.sharding import PartitionSpec as P

BF16, F32 = jnp.bfloat16, jnp.float32
HIGHEST = lax.Precision.HIGHEST
LAST_BY_LAST = (((1,), (1,)), ((), ()))
IN_VMEM = pl.BlockSpec(memory_space=pltpu.VMEM)
IN_HBM = pl.BlockSpec(memory_space=pltpu.HBM)
LANES = 128
CHUNKS = 8
BLOCK = 16
RING = 4
X, Z, Y = 2, 8, 32
CORES = (1, 1)
FAR_FIRST = (2, 3, 1, 0)
WIDTHS = (768, 768, 768, 512, 512, 256)
STARTS = tuple(sum(WIDTHS[:i]) for i in range(len(WIDTHS)))


def on_first_core():
    return lax.rem(lax.axis_index("tensor"), 2) == 0


def place_in_ring():
    index = lax.axis_index("dp")
    return jnp.where(on_first_core(), lax.rem(index, RING), lax.div(index, RING))


def merge_kernel(grads, errors, basis_t, matrix, kept, sent, held, partial, grad_sems, error_sems):
    def copies(i):
        part = (slice(None), pl.ds(STARTS[i], WIDTHS[i]))
        return (
            pltpu.make_async_copy(grads.at[(0, *part)], matrix.at[part], grad_sems.at[i]),
            pltpu.make_async_copy(errors.at[(0, *part)], held.at[part], error_sems.at[i]),
        )

    for i in range(len(WIDTHS)):
        for copy in copies(i):
            copy.start()
    basis_b = basis_t[...].astype(BF16)
    half = kept.shape[1]
    first = on_first_core()
    for i in range(len(WIDTHS)):
        for copy in copies(i):
            copy.wait()
        part = slice(STARTS[i], STARTS[i] + WIDTHS[i])
        total = matrix[:, part] + held[:, part]
        matrix[:, part] = total
        product = lax.dot_general(basis_b[:, part], total, LAST_BY_LAST, preferred_element_type=F32)
        if i:
            product = partial[...] + product
        if i < len(WIDTHS) - 1:
            partial[...] = product
    kept[...] = jnp.where(first, product[:, :half], product[:, half:])
    sent[...] = jnp.where(first, product[:, half:], product[:, :half])


def merge(grads, errors, basis_t):
    rows, cols = grads.shape[1:]
    rank = basis_t.shape[0]
    return pl.pallas_call(
        merge_kernel,
        out_shape=(
            jax.ShapeDtypeStruct((rows, cols), BF16),
            jax.ShapeDtypeStruct((rank, rows // 2), F32),
            jax.ShapeDtypeStruct((rank, rows // 2), F32),
        ),
        in_specs=[IN_HBM, IN_HBM, IN_VMEM],
        out_specs=(IN_VMEM,) * 3,
        scratch_shapes=[
            pltpu.VMEM((rows, cols), BF16),
            pltpu.VMEM((rank, rows), F32),
            pltpu.SemaphoreType.DMA((len(WIDTHS),)),
            pltpu.SemaphoreType.DMA((len(WIDTHS),)),
        ],
        compiler_params=pltpu.CompilerParams(vmem_limit_bytes=44 << 20),
        name="merge",
    )(grads, errors, basis_t)


def inverse_factor(gram):
    rank = gram.shape[0]
    row = lax.broadcasted_iota(jnp.int32, (rank, LANES), 0)
    lane = lax.broadcasted_iota(jnp.int32, (rank, LANES), 1)
    work = jnp.concatenate([gram, jnp.zeros((rank, LANES - rank), F32)], axis=1)
    work = work + jnp.where(lane == row + rank, 1.0, 0.0)
    scale = jnp.zeros((rank, LANES), F32)
    for k in range(0, rank, BLOCK):
        columns = [jnp.broadcast_to(work[:, k + p : k + p + 1], (rank, LANES)) for p in range(BLOCK)]
        lines = [work[k + p : k + p + 1, :] for p in range(BLOCK)]
        scaled = []
        for p in range(BLOCK):
            pivot = columns[p][k + p : k + p + 1, :]
            inverse = 1.0 / pivot
            for q in range(p + 1, BLOCK):
                factor = columns[p][k + q : k + q + 1, :] * inverse
                lines[q] = lines[q] - factor * lines[p]
                columns[q] = columns[q] - factor * columns[p]
            scale = jnp.where(row == k + p, pivot, scale)
            work = jnp.where(row == k + p, lines[p], work)
            scaled.append(lines[p] * inverse)
        for p in range(BLOCK):
            work = work - jnp.where(row >= k + BLOCK, columns[p], 0.0) * scaled[p]
    return (work * lax.rsqrt(scale))[:, rank : 2 * rank]


def project_kernel(mine, other, matrix, p_own, p_b, *refs):
    *q_parts, whole = refs
    rank, half = mine.shape
    first = on_first_core()
    whole[:, :half] = jnp.where(first, mine[...], other[...])
    whole[:, half:] = jnp.where(first, other[...], mine[...])
    p_sum = whole[...]
    gram = lax.dot_general(p_sum, p_sum, LAST_BY_LAST, precision=HIGHEST, preferred_element_type=F32)
    inverse = inverse_factor(gram)
    own = whole[:, pl.ds(pl.multiple_of(lax.axis_index("tensor") * LANES, LANES), LANES)]
    p_own[...] = jnp.dot(inverse, own, precision=HIGHEST, preferred_element_type=F32)
    rounded = jnp.dot(inverse, p_sum, precision=HIGHEST, preferred_element_type=F32).astype(BF16)
    p_b[...] = rounded
    width = q_parts[0].shape[1]
    position = place_in_ring()
    for distance in FAR_FIRST:
        cols = pl.ds(pl.multiple_of((position ^ distance) * width, LANES), width)
        product = jnp.dot(rounded, matrix[:, cols], preferred_element_type=F32)
        q_parts[distance][...] = product.astype(BF16)


def project(mine, other, matrix):
    rank = mine.shape[0]
    rows, cols = matrix.shape
    return pl.pallas_call(
        project_kernel,
        out_shape=(
            jax.ShapeDtypeStruct((rank, LANES), F32),
            jax.ShapeDtypeStruct((rank, rows), BF16),
            *[jax.ShapeDtypeStruct((rank, cols // RING), BF16)] * RING,
        ),
        in_specs=[IN_VMEM] * 3,
        out_specs=(IN_VMEM,) * (2 + RING),
        scratch_shapes=[pltpu.VMEM((rank, rows), F32)],
        compiler_params=pltpu.CompilerParams(vmem_limit_bytes=24 << 20),
        name="project",
    )(mine, other, matrix)


def subtract_kernel(mean, distances, *refs):
    q_parts, (p_b, matrix) = refs[: len(distances)], refs[len(distances) : len(distances) + 2]
    new_errors, q_out, out_buf, q_buf, sems, q_sems = refs[-6:]
    width = q_parts[0].shape[1]
    rows = matrix.shape[0]
    step = rows // CHUNKS
    position = place_in_ring()
    left = p_b[...].T
    copies = []
    for n, distance in enumerate(distances):
        cols = pl.ds(pl.multiple_of((position ^ distance) * width, LANES), width)
        q_buf[n] = q_parts[n][...].astype(F32) * mean
        copies.append(pltpu.make_async_copy(q_buf.at[n], q_out.at[:, cols], q_sems.at[n]))
        copies[-1].start()
        q_b = q_buf[n].astype(BF16)
        for i in range(CHUNKS):
            part = pl.ds(i * step, step)
            approx = jnp.dot(left[i * step : (i + 1) * step], q_b, preferred_element_type=F32)
            out_buf[n, part, :] = (matrix[part, cols].astype(F32) - approx).astype(BF16)
            copies.append(
                pltpu.make_async_copy(out_buf.at[n, part], new_errors.at[0, part, cols], sems.at[n, i])
            )
            copies[-1].start()
    for copy in copies:
        copy.wait()


def subtract(q_parts, p_b, matrix, mean, distances, earlier):
    rows, cols = matrix.shape
    rank, width = q_parts[0].shape
    count = len(q_parts)
    size = count * rows * width
    return pl.pallas_call(
        functools.partial(subtract_kernel, mean, distances),
        out_shape=(
            jax.ShapeDtypeStruct((1, rows, cols), BF16),
            jax.ShapeDtypeStruct((rank, cols), F32),
        ),
        in_specs=[IN_VMEM] * (count + 2) + [IN_HBM] * len(earlier),
        out_specs=(IN_HBM, IN_HBM),
        scratch_shapes=[
            pltpu.VMEM((count, rows, width), BF16),
            pltpu.VMEM((count, rank, width), F32),
            pltpu.SemaphoreType.DMA((count, CHUNKS)),
            pltpu.SemaphoreType.DMA((count,)),
        ],
        input_output_aliases={count + 2: 0, count + 3: 1} if earlier else {},
        compiler_params=pltpu.CompilerParams(vmem_limit_bytes=12 << 20),
        cost_estimate=pl.CostEstimate(flops=2 * size * rank, bytes_accessed=2 * size, transcendentals=0),
        name="subtract",
    )(*q_parts, p_b, matrix, *earlier)


def added_kernel(*refs):
    terms = [ref[...].astype(F32) for ref in refs[:-1]]
    while len(terms) > 1:
        terms = [terms[i] + terms[i + 1] for i in range(0, len(terms), 2)]
    refs[-1][...] = terms[0].astype(refs[-1].dtype)


def added(*terms):
    return pl.pallas_call(
        added_kernel,
        out_shape=jax.ShapeDtypeStruct(terms[0].shape, terms[0].dtype),
        in_specs=[IN_VMEM] * len(terms),
        out_specs=IN_VMEM,
        compiler_params=pltpu.CompilerParams(vmem_limit_bytes=4 << 20),
        name="added",
    )(*terms)


def swapped(value, strides, distance):
    axes = ("dp", "tensor")
    pairs = [(i, i ^ (distance * strides[i % 2])) for i in range(lax.axis_size(axes))]
    return lax.ppermute(value, axes, pairs)


def summed_over_four(values, strides):
    two, three, one = (swapped(values[distance], strides, distance) for distance in (2, 3, 1))
    return added(two, three, one, values[0])


def on_device(grads, errors, basis):
    matrix, kept, sent = merge(grads, errors, basis.T)
    mine = added(kept, swapped(sent, CORES, 1))
    for strides in ((X, Y), (Y, Z), (Z, X)):
        mine = summed_over_four([mine] * RING, strides)
    p_own, p_b, *q_parts = project(mine, swapped(mine, CORES, 1), matrix)
    q_sum = summed_over_four(q_parts, (Z, Y))
    q_sum = summed_over_four([q_sum] * RING, (Y, Z))
    mean, earlier = 1.0 / lax.axis_size("dp"), ()
    for distances in ((0,), (2,), (3, 1)):
        q_now = [swapped(q_sum, (Z, Y), distance) if distance else q_sum for distance in distances]
        earlier = subtract(q_now, p_b, matrix, mean, distances, earlier)
    new_errors, q_out = earlier
    return new_errors, p_own.T, q_out.T


def solution(mesh):
    return jax.shard_map(
        on_device,
        mesh=mesh,
        in_specs=(P("dp", None, "tensor"), P("dp", None, "tensor"), P("tensor", None)),
        out_specs=(P("dp", None, "tensor"), P("tensor", None), P("tensor", None)),
        check_vma=False,
    )
```

```python
import functools

import jax
import jax.numpy as jnp
from jax import lax
from jax.experimental import pallas as pl
from jax.experimental.pallas import tpu as pltpu
from jax.sharding import PartitionSpec as P

BF16, F32 = jnp.bfloat16, jnp.float32
HIGHEST = lax.Precision.HIGHEST
LAST_BY_LAST = (((1,), (1,)), ((), ()))
IN_VMEM = pl.BlockSpec(memory_space=pltpu.VMEM)
IN_HBM = pl.BlockSpec(memory_space=pltpu.HBM)
LANES = 128
CHUNKS = 8
BLOCK = 16
RING = 4
FAR_FIRST = (2, 3, 1, 0)
WIDTHS = (768, 768, 768, 512, 512, 256)
STARTS = tuple(sum(WIDTHS[:i]) for i in range(len(WIDTHS)))


def on_first_core():
    return lax.rem(lax.axis_index("tensor"), 2) == 0


def merge_kernel(grads, errors, basis_t, matrix, kept, sent, held, partial, grad_sems, error_sems):
    def copies(i):
        part = (slice(None), pl.ds(STARTS[i], WIDTHS[i]))
        return (
            pltpu.make_async_copy(grads.at[(0, *part)], matrix.at[part], grad_sems.at[i]),
            pltpu.make_async_copy(errors.at[(0, *part)], held.at[part], error_sems.at[i]),
        )

    for i in range(len(WIDTHS)):
        for copy in copies(i):
            copy.start()
    basis_b = basis_t[...]
    half = kept.shape[1]
    first = on_first_core()
    for i in range(len(WIDTHS)):
        for copy in copies(i):
            copy.wait()
        part = slice(STARTS[i], STARTS[i] + WIDTHS[i])
        total = matrix[:, part] + held[:, part]
        matrix[:, part] = total
        product = lax.dot_general(basis_b[:, part], total, LAST_BY_LAST, preferred_element_type=F32)
        if i:
            product = partial[...] + product
        if i < len(WIDTHS) - 1:
            partial[...] = product
    kept[...] = jnp.where(first, product[:, :half], product[:, half:])
    sent[...] = jnp.where(first, product[:, half:], product[:, :half])


def merge(grads, errors, basis_t):
    rows, cols = grads.shape[1:]
    rank = basis_t.shape[0]
    return pl.pallas_call(
        merge_kernel,
        out_shape=(
            jax.ShapeDtypeStruct((rows, cols), BF16),
            jax.ShapeDtypeStruct((rank, rows // 2), F32),
            jax.ShapeDtypeStruct((rank, rows // 2), F32),
        ),
        in_specs=[IN_HBM, IN_HBM, IN_VMEM],
        out_specs=(IN_VMEM,) * 3,
        scratch_shapes=[
            pltpu.VMEM((rows, cols), BF16),
            pltpu.VMEM((rank, rows), F32),
            pltpu.SemaphoreType.DMA((len(WIDTHS),)),
            pltpu.SemaphoreType.DMA((len(WIDTHS),)),
        ],
        compiler_params=pltpu.CompilerParams(vmem_limit_bytes=44 << 20),
        name="merge",
    )(grads, errors, basis_t)


def inverse_factor(gram):
    rank = gram.shape[0]
    row = lax.broadcasted_iota(jnp.int32, (rank, LANES), 0)
    lane = lax.broadcasted_iota(jnp.int32, (rank, LANES), 1)
    work = jnp.concatenate([gram, jnp.zeros((rank, LANES - rank), F32)], axis=1)
    work = work + jnp.where(lane == row + rank, 1.0, 0.0)
    scale = jnp.zeros((rank, LANES), F32)
    for k in range(0, rank, BLOCK):
        columns = [jnp.broadcast_to(work[:, k + p : k + p + 1], (rank, LANES)) for p in range(BLOCK)]
        lines = [work[k + p : k + p + 1, :] for p in range(BLOCK)]
        scaled = []
        for p in range(BLOCK):
            pivot = columns[p][k + p : k + p + 1, :]
            inverse = 1.0 / pivot
            for q in range(p + 1, BLOCK):
                factor = columns[p][k + q : k + q + 1, :] * inverse
                lines[q] = lines[q] - factor * lines[p]
                columns[q] = columns[q] - factor * columns[p]
            scale = jnp.where(row == k + p, pivot, scale)
            work = jnp.where(row == k + p, lines[p], work)
            scaled.append(lines[p] * inverse)
        for p in range(BLOCK):
            work = work - jnp.where(row >= k + BLOCK, columns[p], 0.0) * scaled[p]
    return (work * lax.rsqrt(scale))[:, rank : 2 * rank]


def project_kernel(mine, other, matrix, p_own, p_b, *refs):
    *q_parts, whole = refs
    rank, half = mine.shape
    first = on_first_core()
    whole[:, :half] = jnp.where(first, mine[...], other[...])
    whole[:, half:] = jnp.where(first, other[...], mine[...])
    p_sum = whole[...]
    gram = lax.dot_general(p_sum, p_sum, LAST_BY_LAST, precision=HIGHEST, preferred_element_type=F32)
    inverse = inverse_factor(gram)
    own = whole[:, pl.ds(pl.multiple_of(lax.axis_index("tensor") * LANES, LANES), LANES)]
    p_own[...] = jnp.dot(inverse, own, precision=HIGHEST, preferred_element_type=F32)
    rounded = jnp.dot(inverse, p_sum, precision=HIGHEST, preferred_element_type=F32).astype(BF16)
    p_b[...] = rounded
    width = q_parts[0].shape[1]
    position = lax.rem(lax.axis_index("dp"), RING)
    for distance in FAR_FIRST:
        cols = pl.ds(pl.multiple_of((position ^ distance) * width, LANES), width)
        product = jnp.dot(rounded, matrix[:, cols], preferred_element_type=F32)
        q_parts[distance][...] = product.astype(BF16)


def project(mine, other, matrix):
    rank = mine.shape[0]
    rows, cols = matrix.shape
    return pl.pallas_call(
        project_kernel,
        out_shape=(
            jax.ShapeDtypeStruct((rank, LANES), F32),
            jax.ShapeDtypeStruct((rank, rows), BF16),
            *[jax.ShapeDtypeStruct((rank, cols // RING), BF16)] * RING,
        ),
        in_specs=[IN_VMEM] * 3,
        out_specs=(IN_VMEM,) * (2 + RING),
        scratch_shapes=[pltpu.VMEM((rank, rows), F32)],
        compiler_params=pltpu.CompilerParams(vmem_limit_bytes=24 << 20),
        name="project",
    )(mine, other, matrix)


def subtract_kernel(mean, distances, *refs):
    q_parts, (p_b, matrix) = refs[: len(distances)], refs[len(distances) : len(distances) + 2]
    new_errors, q_out, out_buf, q_buf, sems, q_sems = refs[-6:]
    width = q_parts[0].shape[1]
    rows = matrix.shape[0]
    step = rows // CHUNKS
    position = lax.rem(lax.axis_index("dp"), RING)
    left = p_b[...].T
    copies = []
    for n, distance in enumerate(distances):
        cols = pl.ds(pl.multiple_of((position ^ distance) * width, LANES), width)
        q_buf[n] = q_parts[n][...].astype(F32) * mean
        copies.append(pltpu.make_async_copy(q_buf.at[n], q_out.at[:, cols], q_sems.at[n]))
        copies[-1].start()
        q_b = q_buf[n].astype(BF16)
        for i in range(CHUNKS):
            part = pl.ds(i * step, step)
            approx = jnp.dot(left[i * step : (i + 1) * step], q_b, preferred_element_type=F32)
            out_buf[n, part, :] = (matrix[part, cols].astype(F32) - approx).astype(BF16)
            copies.append(
                pltpu.make_async_copy(out_buf.at[n, part], new_errors.at[0, part, cols], sems.at[n, i])
            )
            copies[-1].start()
    for copy in copies:
        copy.wait()


def subtract(q_parts, p_b, matrix, mean, distances, earlier):
    rows, cols = matrix.shape
    rank, width = q_parts[0].shape
    count = len(q_parts)
    size = count * rows * width
    return pl.pallas_call(
        functools.partial(subtract_kernel, mean, distances),
        out_shape=(
            jax.ShapeDtypeStruct((1, rows, cols), BF16),
            jax.ShapeDtypeStruct((rank, cols), F32),
        ),
        in_specs=[IN_VMEM] * (count + 2) + [IN_HBM] * len(earlier),
        out_specs=(IN_HBM, IN_HBM),
        scratch_shapes=[
            pltpu.VMEM((count, rows, width), BF16),
            pltpu.VMEM((count, rank, width), F32),
            pltpu.SemaphoreType.DMA((count, CHUNKS)),
            pltpu.SemaphoreType.DMA((count,)),
        ],
        input_output_aliases={count + 2: 0, count + 3: 1} if earlier else {},
        compiler_params=pltpu.CompilerParams(vmem_limit_bytes=12 << 20),
        cost_estimate=pl.CostEstimate(flops=2 * size * rank, bytes_accessed=2 * size, transcendentals=0),
        name="subtract",
    )(*q_parts, p_b, matrix, *earlier)


def added_kernel(*refs):
    terms = [ref[...].astype(F32) for ref in refs[:-1]]
    while len(terms) > 1:
        terms = [terms[i] + terms[i + 1] for i in range(0, len(terms), 2)]
    refs[-1][...] = terms[0].astype(refs[-1].dtype)


def added(*terms):
    return pl.pallas_call(
        added_kernel,
        out_shape=jax.ShapeDtypeStruct(terms[0].shape, terms[0].dtype),
        in_specs=[IN_VMEM] * len(terms),
        out_specs=IN_VMEM,
        compiler_params=pltpu.CompilerParams(vmem_limit_bytes=4 << 20),
        name="added",
    )(*terms)


def swapped(value, axis, stride, distance):
    return lax.ppermute(value, axis, [(i, i ^ (distance * stride)) for i in range(lax.axis_size(axis))])


def summed_over_four(value, axis, stride):
    one, three, two = (swapped(value, axis, stride, distance) for distance in (1, 3, 2))
    return added(two, three, one, value)


def on_device(grads, errors, basis):
    matrix, kept, sent = merge(grads, errors, basis.T.astype(BF16))
    mine = added(kept, swapped(sent, "tensor", 1, 1))
    mine = summed_over_four(mine, "tensor", 2)
    mine = summed_over_four(mine, "dp", 4)
    mine = summed_over_four(mine, "dp", 1)
    p_own, p_b, *q_parts = project(mine, swapped(mine, "tensor", 1, 1), matrix)
    one, three, two = (swapped(q_parts[distance], "dp", 1, distance) for distance in (1, 3, 2))
    q_sum = summed_over_four(added(two, three, one, q_parts[0]), "dp", 4)
    mean, earlier = 1.0 / lax.axis_size("dp"), ()
    for distances in ((0,), (2,), (3, 1)):
        q_now = [swapped(q_sum, "dp", 1, distance) if distance else q_sum for distance in distances]
        earlier = subtract(q_now, p_b, matrix, mean, distances, earlier)
    new_errors, q_out = earlier
    return new_errors, p_own.T, q_out.T


def solution(mesh):
    return jax.shard_map(
        on_device,
        mesh=mesh,
        in_specs=(P("dp", None, "tensor"), P("dp", None, "tensor"), P("tensor", None)),
        out_specs=(P("dp", None, "tensor"), P("tensor", None), P("tensor", None)),
        check_vma=False,
    )
```

```python
import functools

import jax
import jax.numpy as jnp
from jax import lax
from jax.experimental import pallas as pl
from jax.experimental.pallas import tpu as pltpu
from jax.sharding import PartitionSpec as P

BF16, F32 = jnp.bfloat16, jnp.float32
HIGHEST = lax.Precision.HIGHEST
LAST_BY_LAST = (((1,), (1,)), ((), ()))
IN_VMEM = pl.BlockSpec(memory_space=pltpu.VMEM)
IN_HBM = pl.BlockSpec(memory_space=pltpu.HBM)
LANES = 128
CHUNKS = 8
BLOCK = 16
RING = 4
FAR_FIRST = (2, 3, 1, 0)
WIDTHS = (256, 768, 768, 768, 512, 512)
STARTS = tuple(sum(WIDTHS[:i]) for i in range(len(WIDTHS)))


def on_first_core():
    return lax.rem(lax.axis_index("tensor"), 2) == 0


def chunk_copies(grads, errors, matrix, held, grad_sems, error_sems, i):
    part = (slice(None), pl.ds(STARTS[i], WIDTHS[i]))
    return (
        pltpu.make_async_copy(grads.at[(0, *part)], matrix.at[part], grad_sems.at[i]),
        pltpu.make_async_copy(errors.at[(0, *part)], held.at[part], error_sems.at[i]),
    )


def begin_kernel(grads, errors, matrix, held, grad_sems, error_sems):
    copies = chunk_copies(grads, errors, matrix, held, grad_sems, error_sems, 0)
    for copy in copies:
        copy.start()
    for copy in copies:
        copy.wait()
    matrix[:, : WIDTHS[0]] = matrix[:, : WIDTHS[0]] + held[:, : WIDTHS[0]]


def merge_kernel(grads, errors, basis_t, begun, matrix, kept, sent, held, partial, grad_sems, error_sems):
    later = range(1, len(WIDTHS))
    for i in later:
        for copy in chunk_copies(grads, errors, matrix, held, grad_sems, error_sems, i):
            copy.start()
    basis_b = basis_t[...].astype(BF16)
    half = kept.shape[1]
    first = on_first_core()
    begun_part = begun[:, : WIDTHS[0]]
    partial[...] = lax.dot_general(basis_b[:, : WIDTHS[0]], begun_part, LAST_BY_LAST, preferred_element_type=F32)
    for i in later:
        for copy in chunk_copies(grads, errors, matrix, held, grad_sems, error_sems, i):
            copy.wait()
        part = slice(STARTS[i], STARTS[i] + WIDTHS[i])
        total = matrix[:, part] + held[:, part]
        matrix[:, part] = total
        product = lax.dot_general(basis_b[:, part], total, LAST_BY_LAST, preferred_element_type=F32)
        product = partial[...] + product
        if i < len(WIDTHS) - 1:
            partial[...] = product
    kept[...] = jnp.where(first, product[:, :half], product[:, half:])
    sent[...] = jnp.where(first, product[:, half:], product[:, :half])


def merge(grads, errors, basis_t):
    rows, cols = grads.shape[1:]
    rank = basis_t.shape[0]
    whole = jax.ShapeDtypeStruct((rows, cols), BF16)
    half = jax.ShapeDtypeStruct((rank, rows // 2), F32)
    sems = [pltpu.SemaphoreType.DMA((len(WIDTHS),))] * 2
    params = pltpu.CompilerParams(vmem_limit_bytes=44 << 20)
    begun = pl.pallas_call(
        begin_kernel,
        out_shape=whole,
        in_specs=[IN_HBM] * 2,
        out_specs=IN_VMEM,
        scratch_shapes=[pltpu.VMEM((rows, WIDTHS[0]), BF16), *sems],
        compiler_params=params,
        cost_estimate=pl.CostEstimate(flops=rows * WIDTHS[0], bytes_accessed=4 * rows * WIDTHS[0], transcendentals=0),
        name="begin",
    )(grads, errors)
    return pl.pallas_call(
        merge_kernel,
        out_shape=(whole, half, half),
        in_specs=[IN_HBM, IN_HBM, IN_VMEM, IN_VMEM],
        out_specs=(IN_VMEM,) * 3,
        scratch_shapes=[pltpu.VMEM((rows, cols), BF16), pltpu.VMEM((rank, rows), F32), *sems],
        input_output_aliases={3: 0},
        compiler_params=params,
        name="merge",
    )(grads, errors, basis_t, begun)


def inverse_factor(gram):
    rank = gram.shape[0]
    row = lax.broadcasted_iota(jnp.int32, (rank, LANES), 0)
    lane = lax.broadcasted_iota(jnp.int32, (rank, LANES), 1)
    work = jnp.concatenate([gram, jnp.zeros((rank, LANES - rank), F32)], axis=1)
    work = work + jnp.where(lane == row + rank, 1.0, 0.0)
    scale = jnp.zeros((rank, LANES), F32)
    for k in range(0, rank, BLOCK):
        columns = [jnp.broadcast_to(work[:, k + p : k + p + 1], (rank, LANES)) for p in range(BLOCK)]
        lines = [work[k + p : k + p + 1, :] for p in range(BLOCK)]
        scaled = []
        for p in range(BLOCK):
            pivot = columns[p][k + p : k + p + 1, :]
            inverse = 1.0 / pivot
            for q in range(p + 1, BLOCK):
                factor = columns[p][k + q : k + q + 1, :] * inverse
                lines[q] = lines[q] - factor * lines[p]
                columns[q] = columns[q] - factor * columns[p]
            scale = jnp.where(row == k + p, pivot, scale)
            work = jnp.where(row == k + p, lines[p], work)
            scaled.append(lines[p] * inverse)
        for p in range(BLOCK):
            work = work - jnp.where(row >= k + BLOCK, columns[p], 0.0) * scaled[p]
    return (work * lax.rsqrt(scale))[:, rank : 2 * rank]


def project_kernel(mine, other, matrix, p_own, p_b, *refs):
    *q_parts, whole = refs
    rank, half = mine.shape
    first = on_first_core()
    whole[:, :half] = jnp.where(first, mine[...], other[...])
    whole[:, half:] = jnp.where(first, other[...], mine[...])
    p_sum = whole[...]
    gram = lax.dot_general(p_sum, p_sum, LAST_BY_LAST, precision=HIGHEST, preferred_element_type=F32)
    inverse = inverse_factor(gram)
    own = whole[:, pl.ds(pl.multiple_of(lax.axis_index("tensor") * LANES, LANES), LANES)]
    p_own[...] = jnp.dot(inverse, own, precision=HIGHEST, preferred_element_type=F32)
    rounded = jnp.dot(inverse, p_sum, precision=HIGHEST, preferred_element_type=F32).astype(BF16)
    p_b[...] = rounded
    width = q_parts[0].shape[1]
    position = lax.rem(lax.axis_index("dp"), RING)
    for distance in FAR_FIRST:
        cols = pl.ds(pl.multiple_of((position ^ distance) * width, LANES), width)
        product = jnp.dot(rounded, matrix[:, cols], preferred_element_type=F32)
        q_parts[distance][...] = product.astype(BF16)


def project(mine, other, matrix):
    rank = mine.shape[0]
    rows, cols = matrix.shape
    return pl.pallas_call(
        project_kernel,
        out_shape=(
            jax.ShapeDtypeStruct((rank, LANES), F32),
            jax.ShapeDtypeStruct((rank, rows), BF16),
            *[jax.ShapeDtypeStruct((rank, cols // RING), BF16)] * RING,
        ),
        in_specs=[IN_VMEM] * 3,
        out_specs=(IN_VMEM,) * (2 + RING),
        scratch_shapes=[pltpu.VMEM((rank, rows), F32)],
        compiler_params=pltpu.CompilerParams(vmem_limit_bytes=24 << 20),
        name="project",
    )(mine, other, matrix)


def subtract_kernel(mean, distances, *refs):
    q_parts, (p_b, matrix) = refs[: len(distances)], refs[len(distances) : len(distances) + 2]
    new_errors, q_out, out_buf, q_buf, sems, q_sems = refs[-6:]
    width = q_parts[0].shape[1]
    rows = matrix.shape[0]
    step = rows // CHUNKS
    position = lax.rem(lax.axis_index("dp"), RING)
    left = p_b[...].T
    copies = []
    for n, distance in enumerate(distances):
        cols = pl.ds(pl.multiple_of((position ^ distance) * width, LANES), width)
        q_buf[n] = q_parts[n][...].astype(F32) * mean
        copies.append(pltpu.make_async_copy(q_buf.at[n], q_out.at[:, cols], q_sems.at[n]))
        copies[-1].start()
        q_b = q_buf[n].astype(BF16)
        for i in range(CHUNKS):
            part = pl.ds(i * step, step)
            approx = jnp.dot(left[i * step : (i + 1) * step], q_b, preferred_element_type=F32)
            out_buf[n, part, :] = (matrix[part, cols].astype(F32) - approx).astype(BF16)
            copies.append(
                pltpu.make_async_copy(out_buf.at[n, part], new_errors.at[0, part, cols], sems.at[n, i])
            )
            copies[-1].start()
    for copy in copies:
        copy.wait()


def subtract(q_parts, p_b, matrix, mean, distances, earlier):
    rows, cols = matrix.shape
    rank, width = q_parts[0].shape
    count = len(q_parts)
    size = count * rows * width
    return pl.pallas_call(
        functools.partial(subtract_kernel, mean, distances),
        out_shape=(
            jax.ShapeDtypeStruct((1, rows, cols), BF16),
            jax.ShapeDtypeStruct((rank, cols), F32),
        ),
        in_specs=[IN_VMEM] * (count + 2) + [IN_HBM] * len(earlier),
        out_specs=(IN_HBM, IN_HBM),
        scratch_shapes=[
            pltpu.VMEM((count, rows, width), BF16),
            pltpu.VMEM((count, rank, width), F32),
            pltpu.SemaphoreType.DMA((count, CHUNKS)),
            pltpu.SemaphoreType.DMA((count,)),
        ],
        input_output_aliases={count + 2: 0, count + 3: 1} if earlier else {},
        compiler_params=pltpu.CompilerParams(vmem_limit_bytes=12 << 20),
        cost_estimate=pl.CostEstimate(flops=2 * size * rank, bytes_accessed=2 * size, transcendentals=0),
        name="subtract",
    )(*q_parts, p_b, matrix, *earlier)


def added_kernel(*refs):
    terms = [ref[...].astype(F32) for ref in refs[:-1]]
    while len(terms) > 1:
        terms = [terms[i] + terms[i + 1] for i in range(0, len(terms), 2)]
    refs[-1][...] = terms[0].astype(refs[-1].dtype)


def added(*terms):
    return pl.pallas_call(
        added_kernel,
        out_shape=jax.ShapeDtypeStruct(terms[0].shape, terms[0].dtype),
        in_specs=[IN_VMEM] * len(terms),
        out_specs=IN_VMEM,
        compiler_params=pltpu.CompilerParams(vmem_limit_bytes=4 << 20),
        name="added",
    )(*terms)


def swapped(value, axis, stride, distance):
    return lax.ppermute(value, axis, [(i, i ^ (distance * stride)) for i in range(lax.axis_size(axis))])


def summed_over_four(value, axis, stride):
    one, three, two = (swapped(value, axis, stride, distance) for distance in (1, 3, 2))
    return added(two, three, one, value)


def on_device(grads, errors, basis):
    matrix, kept, sent = merge(grads, errors, basis.T)
    mine = added(kept, swapped(sent, "tensor", 1, 1))
    mine = summed_over_four(mine, "tensor", 2)
    mine = summed_over_four(mine, "dp", 4)
    mine = summed_over_four(mine, "dp", 1)
    p_own, p_b, *q_parts = project(mine, swapped(mine, "tensor", 1, 1), matrix)
    one, three, two = (swapped(q_parts[distance], "dp", 1, distance) for distance in (1, 3, 2))
    q_sum = summed_over_four(added(two, three, one, q_parts[0]), "dp", 4)
    mean, earlier = 1.0 / lax.axis_size("dp"), ()
    for distances in ((0,), (2,), (3, 1)):
        q_now = [swapped(q_sum, "dp", 1, distance) if distance else q_sum for distance in distances]
        earlier = subtract(q_now, p_b, matrix, mean, distances, earlier)
    new_errors, q_out = earlier
    return new_errors, p_own.T, q_out.T


def solution(mesh):
    return jax.shard_map(
        on_device,
        mesh=mesh,
        in_specs=(P("dp", None, "tensor"), P("dp", None, "tensor"), P("tensor", None)),
        out_specs=(P("dp", None, "tensor"), P("tensor", None), P("tensor", None)),
        check_vma=False,
    )
```

```python
import functools

import jax
import jax.numpy as jnp
from jax import lax
from jax.experimental import pallas as pl
from jax.experimental.pallas import tpu as pltpu
from jax.sharding import PartitionSpec as P

BF16, F32 = jnp.bfloat16, jnp.float32
HIGHEST = lax.Precision.HIGHEST
LAST_BY_LAST = (((1,), (1,)), ((), ()))
IN_VMEM = pl.BlockSpec(memory_space=pltpu.VMEM)
IN_HBM = pl.BlockSpec(memory_space=pltpu.HBM)
LANES = 128
CHUNKS = 8
BLOCK = 16
RING = 4
EARLY, LATE = (2, 3, 1), (0,)
WIDTHS = (768, 768, 768, 512, 512, 256)
STARTS = tuple(sum(WIDTHS[:i]) for i in range(len(WIDTHS)))


def on_first_core():
    return lax.rem(lax.axis_index("tensor"), 2) == 0


def merge_kernel(grads, errors, basis_t, matrix, kept, sent, held, partial, grad_sems, error_sems):
    def copies(i):
        part = (slice(None), pl.ds(STARTS[i], WIDTHS[i]))
        return (
            pltpu.make_async_copy(grads.at[(0, *part)], matrix.at[part], grad_sems.at[i]),
            pltpu.make_async_copy(errors.at[(0, *part)], held.at[part], error_sems.at[i]),
        )

    for i in range(len(WIDTHS)):
        for copy in copies(i):
            copy.start()
    basis_b = basis_t[...].astype(BF16)
    half = kept.shape[1]
    first = on_first_core()
    for i in range(len(WIDTHS)):
        for copy in copies(i):
            copy.wait()
        part = slice(STARTS[i], STARTS[i] + WIDTHS[i])
        total = matrix[:, part] + held[:, part]
        matrix[:, part] = total
        product = lax.dot_general(basis_b[:, part], total, LAST_BY_LAST, preferred_element_type=F32)
        if i:
            product = partial[...] + product
        if i < len(WIDTHS) - 1:
            partial[...] = product
    kept[...] = jnp.where(first, product[:, :half], product[:, half:])
    sent[...] = jnp.where(first, product[:, half:], product[:, :half])


def merge(grads, errors, basis_t):
    rows, cols = grads.shape[1:]
    rank = basis_t.shape[0]
    return pl.pallas_call(
        merge_kernel,
        out_shape=(
            jax.ShapeDtypeStruct((rows, cols), BF16),
            jax.ShapeDtypeStruct((rank, rows // 2), F32),
            jax.ShapeDtypeStruct((rank, rows // 2), F32),
        ),
        in_specs=[IN_HBM, IN_HBM, IN_VMEM],
        out_specs=(IN_VMEM,) * 3,
        scratch_shapes=[
            pltpu.VMEM((rows, cols), BF16),
            pltpu.VMEM((rank, rows), F32),
            pltpu.SemaphoreType.DMA((len(WIDTHS),)),
            pltpu.SemaphoreType.DMA((len(WIDTHS),)),
        ],
        compiler_params=pltpu.CompilerParams(vmem_limit_bytes=44 << 20),
        name="merge",
    )(grads, errors, basis_t)


def inverse_factor(gram):
    rank = gram.shape[0]
    row = lax.broadcasted_iota(jnp.int32, (rank, LANES), 0)
    lane = lax.broadcasted_iota(jnp.int32, (rank, LANES), 1)
    work = jnp.concatenate([gram, jnp.zeros((rank, LANES - rank), F32)], axis=1)
    work = work + jnp.where(lane == row + rank, 1.0, 0.0)
    scale = jnp.zeros((rank, LANES), F32)
    for k in range(0, rank, BLOCK):
        columns = [jnp.broadcast_to(work[:, k + p : k + p + 1], (rank, LANES)) for p in range(BLOCK)]
        lines = [work[k + p : k + p + 1, :] for p in range(BLOCK)]
        scaled = []
        for p in range(BLOCK):
            pivot = columns[p][k + p : k + p + 1, :]
            inverse = 1.0 / pivot
            for q in range(p + 1, BLOCK):
                factor = columns[p][k + q : k + q + 1, :] * inverse
                lines[q] = lines[q] - factor * lines[p]
                columns[q] = columns[q] - factor * columns[p]
            scale = jnp.where(row == k + p, pivot, scale)
            work = jnp.where(row == k + p, lines[p], work)
            scaled.append(lines[p] * inverse)
        for p in range(BLOCK):
            work = work - jnp.where(row >= k + BLOCK, columns[p], 0.0) * scaled[p]
    return (work * lax.rsqrt(scale))[:, rank : 2 * rank]


def project_kernel(mine, other, matrix, p_own, p_b, *refs):
    *q_parts, whole = refs
    rank, half = mine.shape
    first = on_first_core()
    whole[:, :half] = jnp.where(first, mine[...], other[...])
    whole[:, half:] = jnp.where(first, other[...], mine[...])
    p_sum = whole[...]
    gram = lax.dot_general(p_sum, p_sum, LAST_BY_LAST, precision=HIGHEST, preferred_element_type=F32)
    inverse = inverse_factor(gram)
    own = whole[:, pl.ds(pl.multiple_of(lax.axis_index("tensor") * LANES, LANES), LANES)]
    p_own[...] = jnp.dot(inverse, own, precision=HIGHEST, preferred_element_type=F32)
    rounded = jnp.dot(inverse, p_sum, precision=HIGHEST, preferred_element_type=F32).astype(BF16)
    p_b[...] = rounded
    quarters(rounded, matrix, EARLY, q_parts)


def quarters(left, matrix, distances, q_parts):
    width = q_parts[0].shape[1]
    position = lax.rem(lax.axis_index("dp"), RING)
    for distance, q_part in zip(distances, q_parts):
        cols = pl.ds(pl.multiple_of((position ^ distance) * width, LANES), width)
        q_part[...] = jnp.dot(left, matrix[:, cols], preferred_element_type=F32).astype(BF16)


def rest_kernel(p_b, matrix, _, *q_parts):
    quarters(p_b[...], matrix, LATE, q_parts)


def rest(p_b, matrix, arrived):
    rank, (rows, cols) = p_b.shape[0], matrix.shape
    size = rows * cols // RING * len(LATE)
    return pl.pallas_call(
        rest_kernel,
        out_shape=(jax.ShapeDtypeStruct((rank, cols // RING), BF16),) * len(LATE),
        in_specs=[IN_VMEM] * 3,
        out_specs=(IN_VMEM,) * len(LATE),
        compiler_params=pltpu.CompilerParams(vmem_limit_bytes=8 << 20),
        cost_estimate=pl.CostEstimate(flops=2 * size * rank, bytes_accessed=2 * size, transcendentals=0),
        name="rest",
    )(p_b, matrix, arrived)


def project(mine, other, matrix):
    rank = mine.shape[0]
    rows, cols = matrix.shape
    return pl.pallas_call(
        project_kernel,
        out_shape=(
            jax.ShapeDtypeStruct((rank, LANES), F32),
            jax.ShapeDtypeStruct((rank, rows), BF16),
            *[jax.ShapeDtypeStruct((rank, cols // RING), BF16)] * len(EARLY),
        ),
        in_specs=[IN_VMEM] * 3,
        out_specs=(IN_VMEM,) * (2 + len(EARLY)),
        scratch_shapes=[pltpu.VMEM((rank, rows), F32)],
        compiler_params=pltpu.CompilerParams(vmem_limit_bytes=24 << 20),
        name="project",
    )(mine, other, matrix)


def subtract_kernel(mean, distances, *refs):
    q_parts, (p_b, matrix) = refs[: len(distances)], refs[len(distances) : len(distances) + 2]
    new_errors, q_out, out_buf, q_buf, sems, q_sems = refs[-6:]
    width = q_parts[0].shape[1]
    rows = matrix.shape[0]
    step = rows // CHUNKS
    position = lax.rem(lax.axis_index("dp"), RING)
    left = p_b[...].T
    copies = []
    for n, distance in enumerate(distances):
        cols = pl.ds(pl.multiple_of((position ^ distance) * width, LANES), width)
        q_buf[n] = q_parts[n][...].astype(F32) * mean
        copies.append(pltpu.make_async_copy(q_buf.at[n], q_out.at[:, cols], q_sems.at[n]))
        copies[-1].start()
        q_b = q_buf[n].astype(BF16)
        for i in range(CHUNKS):
            part = pl.ds(i * step, step)
            approx = jnp.dot(left[i * step : (i + 1) * step], q_b, preferred_element_type=F32)
            out_buf[n, part, :] = (matrix[part, cols].astype(F32) - approx).astype(BF16)
            copies.append(
                pltpu.make_async_copy(out_buf.at[n, part], new_errors.at[0, part, cols], sems.at[n, i])
            )
            copies[-1].start()
    for copy in copies:
        copy.wait()


def subtract(q_parts, p_b, matrix, mean, distances, earlier):
    rows, cols = matrix.shape
    rank, width = q_parts[0].shape
    count = len(q_parts)
    size = count * rows * width
    return pl.pallas_call(
        functools.partial(subtract_kernel, mean, distances),
        out_shape=(
            jax.ShapeDtypeStruct((1, rows, cols), BF16),
            jax.ShapeDtypeStruct((rank, cols), F32),
        ),
        in_specs=[IN_VMEM] * (count + 2) + [IN_HBM] * len(earlier),
        out_specs=(IN_HBM, IN_HBM),
        scratch_shapes=[
            pltpu.VMEM((count, rows, width), BF16),
            pltpu.VMEM((count, rank, width), F32),
            pltpu.SemaphoreType.DMA((count, CHUNKS)),
            pltpu.SemaphoreType.DMA((count,)),
        ],
        input_output_aliases={count + 2: 0, count + 3: 1} if earlier else {},
        compiler_params=pltpu.CompilerParams(vmem_limit_bytes=12 << 20),
        cost_estimate=pl.CostEstimate(flops=2 * size * rank, bytes_accessed=2 * size, transcendentals=0),
        name="subtract",
    )(*q_parts, p_b, matrix, *earlier)


def added_kernel(*refs):
    terms = [ref[...].astype(F32) for ref in refs[:-1]]
    while len(terms) > 1:
        terms = [terms[i] + terms[i + 1] for i in range(0, len(terms), 2)]
    refs[-1][...] = terms[0].astype(refs[-1].dtype)


def added(*terms):
    return pl.pallas_call(
        added_kernel,
        out_shape=jax.ShapeDtypeStruct(terms[0].shape, terms[0].dtype),
        in_specs=[IN_VMEM] * len(terms),
        out_specs=IN_VMEM,
        compiler_params=pltpu.CompilerParams(vmem_limit_bytes=4 << 20),
        name="added",
    )(*terms)


def swapped(value, axis, stride, distance):
    return lax.ppermute(value, axis, [(i, i ^ (distance * stride)) for i in range(lax.axis_size(axis))])


def summed_over_four(value, axis, stride):
    one, three, two = (swapped(value, axis, stride, distance) for distance in (1, 3, 2))
    return added(two, three, one, value)


def on_device(grads, errors, basis):
    matrix, kept, sent = merge(grads, errors, basis.T)
    mine = added(kept, swapped(sent, "tensor", 1, 1))
    mine = summed_over_four(mine, "tensor", 2)
    mine = summed_over_four(mine, "dp", 4)
    mine = summed_over_four(mine, "dp", 1)
    p_own, p_b, *q_parts = project(mine, swapped(mine, "tensor", 1, 1), matrix)
    two, three, one = (swapped(q_part, "dp", 1, distance) for q_part, distance in zip(q_parts, EARLY))
    (q_own,) = rest(p_b, matrix, two)
    q_sum = summed_over_four(added(two, three, one, q_own), "dp", 4)
    mean, earlier = 1.0 / lax.axis_size("dp"), ()
    for distances in ((0,), (2,), (3, 1)):
        q_now = [swapped(q_sum, "dp", 1, distance) if distance else q_sum for distance in distances]
        earlier = subtract(q_now, p_b, matrix, mean, distances, earlier)
    new_errors, q_out = earlier
    return new_errors, p_own.T, q_out.T


def solution(mesh):
    return jax.shard_map(
        on_device,
        mesh=mesh,
        in_specs=(P("dp", None, "tensor"), P("dp", None, "tensor"), P("tensor", None)),
        out_specs=(P("dp", None, "tensor"), P("tensor", None), P("tensor", None)),
        check_vma=False,
    )
```

```python
import functools

import jax
import jax.numpy as jnp
from jax import lax
from jax.experimental import pallas as pl
from jax.experimental.pallas import tpu as pltpu
from jax.sharding import PartitionSpec as P

BF16, F32 = jnp.bfloat16, jnp.float32
HIGHEST = lax.Precision.HIGHEST
LAST_BY_LAST = (((1,), (1,)), ((), ()))
IN_VMEM = pl.BlockSpec(memory_space=pltpu.VMEM)
IN_HBM = pl.BlockSpec(memory_space=pltpu.HBM)
LANES = 128
CHUNKS = 8
BLOCK = 16
RING = 4
EARLY, LATE = (2, 3, 1), (0,)
WIDTHS = (768, 768, 768, 512, 512, 256)
STARTS = tuple(sum(WIDTHS[:i]) for i in range(len(WIDTHS)))


def on_first_core():
    return lax.rem(lax.axis_index("tensor"), 2) == 0


def merge_kernel(grads, errors, basis_t, matrix, kept, sent, held, partial, grad_sems, error_sems):
    def copies(i):
        part = (slice(None), pl.ds(STARTS[i], WIDTHS[i]))
        return (
            pltpu.make_async_copy(grads.at[(0, *part)], matrix.at[part], grad_sems.at[i]),
            pltpu.make_async_copy(errors.at[(0, *part)], held.at[part], error_sems.at[i]),
        )

    for i in range(len(WIDTHS)):
        for copy in copies(i):
            copy.start()
    basis_b = basis_t[...].astype(BF16)
    half = kept.shape[1]
    first = on_first_core()
    for i in range(len(WIDTHS)):
        for copy in copies(i):
            copy.wait()
        part = slice(STARTS[i], STARTS[i] + WIDTHS[i])
        total = matrix[:, part] + held[:, part]
        matrix[:, part] = total
        product = lax.dot_general(basis_b[:, part], total, LAST_BY_LAST, preferred_element_type=F32)
        if i:
            product = partial[...] + product
        if i < len(WIDTHS) - 1:
            partial[...] = product
    kept[...] = jnp.where(first, product[:, :half], product[:, half:])
    sent[...] = jnp.where(first, product[:, half:], product[:, :half])


def merge(grads, errors, basis_t):
    rows, cols = grads.shape[1:]
    rank = basis_t.shape[0]
    return pl.pallas_call(
        merge_kernel,
        out_shape=(
            jax.ShapeDtypeStruct((rows, cols), BF16),
            jax.ShapeDtypeStruct((rank, rows // 2), F32),
            jax.ShapeDtypeStruct((rank, rows // 2), F32),
        ),
        in_specs=[IN_HBM, IN_HBM, IN_VMEM],
        out_specs=(IN_VMEM,) * 3,
        scratch_shapes=[
            pltpu.VMEM((rows, cols), BF16),
            pltpu.VMEM((rank, rows), F32),
            pltpu.SemaphoreType.DMA((len(WIDTHS),)),
            pltpu.SemaphoreType.DMA((len(WIDTHS),)),
        ],
        compiler_params=pltpu.CompilerParams(vmem_limit_bytes=44 << 20),
        name="merge",
    )(grads, errors, basis_t)


def inverse_factor(gram):
    rank = gram.shape[0]
    row = lax.broadcasted_iota(jnp.int32, (rank, LANES), 0)
    lane = lax.broadcasted_iota(jnp.int32, (rank, LANES), 1)
    work = jnp.concatenate([gram, jnp.zeros((rank, LANES - rank), F32)], axis=1)
    work = work + jnp.where(lane == row + rank, 1.0, 0.0)
    scale = jnp.zeros((rank, LANES), F32)
    for k in range(0, rank, BLOCK):
        columns = [jnp.broadcast_to(work[:, k + p : k + p + 1], (rank, LANES)) for p in range(BLOCK)]
        lines = [work[k + p : k + p + 1, :] for p in range(BLOCK)]
        scaled = []
        for p in range(BLOCK):
            pivot = columns[p][k + p : k + p + 1, :]
            inverse = 1.0 / pivot
            for q in range(p + 1, BLOCK):
                factor = columns[p][k + q : k + q + 1, :] * inverse
                lines[q] = lines[q] - factor * lines[p]
                columns[q] = columns[q] - factor * columns[p]
            scale = jnp.where(row == k + p, pivot, scale)
            work = jnp.where(row == k + p, lines[p], work)
            scaled.append(lines[p] * inverse)
        for p in range(BLOCK):
            work = work - jnp.where(row >= k + BLOCK, columns[p], 0.0) * scaled[p]
    return (work * lax.rsqrt(scale))[:, rank : 2 * rank]


def project_kernel(mine, other, matrix, p_own, p_b, *refs):
    *q_parts, whole = refs
    rank, half = mine.shape
    first = on_first_core()
    whole[:, :half] = jnp.where(first, mine[...], other[...])
    whole[:, half:] = jnp.where(first, other[...], mine[...])
    p_sum = whole[...]
    gram = lax.dot_general(p_sum, p_sum, LAST_BY_LAST, precision=HIGHEST, preferred_element_type=F32)
    inverse = inverse_factor(gram)
    own = whole[:, pl.ds(pl.multiple_of(lax.axis_index("tensor") * LANES, LANES), LANES)]
    p_own[...] = jnp.dot(inverse, own, precision=HIGHEST, preferred_element_type=F32)
    rounded = jnp.dot(inverse, p_sum, precision=HIGHEST, preferred_element_type=F32).astype(BF16)
    p_b[...] = rounded
    quarters(rounded, matrix, EARLY, q_parts)


def quarters(left, matrix, distances, q_parts):
    width = q_parts[0].shape[1]
    position = lax.rem(lax.axis_index("dp"), RING)
    for distance, q_part in zip(distances, q_parts):
        cols = pl.ds(pl.multiple_of((position ^ distance) * width, LANES), width)
        q_part[...] = jnp.dot(left, matrix[:, cols], preferred_element_type=F32).astype(BF16)


def rest_kernel(p_b, matrix, _, *q_parts):
    quarters(p_b[...], matrix, LATE, q_parts)


def rest(p_b, matrix, arrived):
    rank, (rows, cols) = p_b.shape[0], matrix.shape
    size = rows * cols // RING * len(LATE)
    return pl.pallas_call(
        rest_kernel,
        out_shape=(jax.ShapeDtypeStruct((rank, cols // RING), BF16),) * len(LATE),
        in_specs=[IN_VMEM] * 3,
        out_specs=(IN_VMEM,) * len(LATE),
        compiler_params=pltpu.CompilerParams(vmem_limit_bytes=8 << 20),
        cost_estimate=pl.CostEstimate(flops=2 * size * rank, bytes_accessed=2 * size, transcendentals=0),
        name="rest",
    )(p_b, matrix, arrived)


def project(mine, other, matrix):
    rank = mine.shape[0]
    rows, cols = matrix.shape
    return pl.pallas_call(
        project_kernel,
        out_shape=(
            jax.ShapeDtypeStruct((rank, LANES), F32),
            jax.ShapeDtypeStruct((rank, rows), BF16),
            *[jax.ShapeDtypeStruct((rank, cols // RING), BF16)] * len(EARLY),
        ),
        in_specs=[IN_VMEM] * 3,
        out_specs=(IN_VMEM,) * (2 + len(EARLY)),
        scratch_shapes=[pltpu.VMEM((rank, rows), F32)],
        compiler_params=pltpu.CompilerParams(vmem_limit_bytes=24 << 20),
        name="project",
    )(mine, other, matrix)


def subtract_kernel(mean, distances, *refs):
    q_parts, (p_b, matrix) = refs[: len(distances)], refs[len(distances) : len(distances) + 2]
    new_errors, q_out, out_buf, q_buf, sems, q_sems = refs[-6:]
    width = q_parts[0].shape[1]
    rows = matrix.shape[0]
    step = rows // CHUNKS
    position = lax.rem(lax.axis_index("dp"), RING)
    left = p_b[...].T
    copies = []
    for n, distance in enumerate(distances):
        cols = pl.ds(pl.multiple_of((position ^ distance) * width, LANES), width)
        q_buf[n] = q_parts[n][...].astype(F32) * mean
        copies.append(pltpu.make_async_copy(q_buf.at[n], q_out.at[:, cols], q_sems.at[n]))
        copies[-1].start()
        q_b = q_buf[n].astype(BF16)
        for i in range(CHUNKS):
            part = pl.ds(i * step, step)
            approx = jnp.dot(left[i * step : (i + 1) * step], q_b, preferred_element_type=F32)
            out_buf[n, part, :] = (matrix[part, cols].astype(F32) - approx).astype(BF16)
            copies.append(
                pltpu.make_async_copy(out_buf.at[n, part], new_errors.at[0, part, cols], sems.at[n, i])
            )
            copies[-1].start()
    for copy in copies:
        copy.wait()


def subtract(q_parts, p_b, matrix, mean, distances, earlier):
    rows, cols = matrix.shape
    rank, width = q_parts[0].shape
    count = len(q_parts)
    size = count * rows * width
    return pl.pallas_call(
        functools.partial(subtract_kernel, mean, distances),
        out_shape=(
            jax.ShapeDtypeStruct((1, rows, cols), BF16),
            jax.ShapeDtypeStruct((rank, cols), F32),
        ),
        in_specs=[IN_VMEM] * (count + 2) + [IN_HBM] * len(earlier),
        out_specs=(IN_HBM, IN_HBM),
        scratch_shapes=[
            pltpu.VMEM((count, rows, width), BF16),
            pltpu.VMEM((count, rank, width), F32),
            pltpu.SemaphoreType.DMA((count, CHUNKS)),
            pltpu.SemaphoreType.DMA((count,)),
        ],
        input_output_aliases={count + 2: 0, count + 3: 1} if earlier else {},
        compiler_params=pltpu.CompilerParams(vmem_limit_bytes=12 << 20),
        cost_estimate=pl.CostEstimate(flops=2 * size * rank, bytes_accessed=2 * size, transcendentals=0),
        name="subtract",
    )(*q_parts, p_b, matrix, *earlier)


def added_kernel(*refs):
    terms = [ref[...].astype(F32) for ref in refs[:-1]]
    while len(terms) > 1:
        terms = [terms[i] + terms[i + 1] for i in range(0, len(terms), 2)]
    refs[-1][...] = terms[0].astype(refs[-1].dtype)


def added(*terms):
    return pl.pallas_call(
        added_kernel,
        out_shape=jax.ShapeDtypeStruct(terms[0].shape, terms[0].dtype),
        in_specs=[IN_VMEM] * len(terms),
        out_specs=IN_VMEM,
        compiler_params=pltpu.CompilerParams(vmem_limit_bytes=4 << 20),
        name="added",
    )(*terms)


def swapped(value, axis, stride, distance):
    return lax.ppermute(value, axis, [(i, i ^ (distance * stride)) for i in range(lax.axis_size(axis))])


def summed_over_four(value, axis, stride):
    one, three, two = (swapped(value, axis, stride, distance) for distance in (1, 3, 2))
    return added(two, three, one, value)


def on_device(grads, errors, basis):
    matrix, kept, sent = merge(grads, errors, basis.T)
    mine = added(kept, swapped(sent, "tensor", 1, 1))
    mine = summed_over_four(mine, "tensor", 2)
    mine = summed_over_four(mine, "dp", 4)
    mine = summed_over_four(mine, "dp", 1)
    p_own, p_b, *q_parts = project(mine, swapped(mine, "tensor", 1, 1), matrix)
    two, three, one = (swapped(q_part, "dp", 1, distance) for q_part, distance in zip(q_parts, EARLY))
    (q_own,) = rest(p_b, matrix, two)
    q_sum = summed_over_four(added(two, three, one, q_own), "dp", 4)
    mean, earlier = 1.0 / lax.axis_size("dp"), ()
    for distances in ((0,), (2, 1), (3,)):
        q_now = [swapped(q_sum, "dp", 1, distance) if distance else q_sum for distance in distances]
        earlier = subtract(q_now, p_b, matrix, mean, distances, earlier)
    new_errors, q_out = earlier
    return new_errors, p_own.T, q_out.T


def solution(mesh):
    return jax.shard_map(
        on_device,
        mesh=mesh,
        in_specs=(P("dp", None, "tensor"), P("dp", None, "tensor"), P("tensor", None)),
        out_specs=(P("dp", None, "tensor"), P("tensor", None), P("tensor", None)),
        check_vma=False,
    )
```
